32 devices in a mesh: seq: 8 (over y, x, core), tp: 4 (over z).
Axes of the slice: x: 2, y: 2, z: 4, core: 2. Of those that a mesh axis runs over, the one named last changes fastest.
Arguments:
- gate_input: bfloat16 [8192, 8192], P('seq', 'tp'), may hold values from -6 to 6
- key_input: bfloat16 [8192, 8192], P('seq', 'tp'), may hold values from -6 to 6
- value_input: bfloat16 [8192, 8192], P('seq', 'tp'), may hold values from -6 to 6
- filter_taps: bfloat16 [512, 2048], P('tp'), as said below
- out_weight: bfloat16 [4096, 8192], P(None, 'tp'), may hold values from -0.0625 to 0.0625
Outputs:
- mixed: bfloat16 [4096, 8192], P('tp', 'seq')
The draws below stay inside these ranges and needn't reach their ends.
Inputs may be any that keep to these rules, and one draw needn't show every extreme that they name: `filter_taps`: one causal filter for each group of 16 consecutive channels, indexed by lag.
All inputs are finite; a program needn't handle non-finite values.
Results may differ from the reference program's by a relative error of at most 0.0095.
Values may be sent and summed in bfloat16 or wider, within the bound.
A program may use at most 192 MiB of HBM per device.

```python
import math
import jax
import jax.numpy as jnp
from jax import lax

D = 8192
OUT = 4096
GROUP_SIZE = 16
KERNEL_COHORTS = 512
KERNEL_SPAN_TAPS = 2048
TOKENS = 8192
N_TP = 4


def draw_filter_taps(key, part):
    forked_seed_pairs = jax.random.split(key, 5)
    quick_share = 0.5
    amplitude = jax.random.truncated_normal(forked_seed_pairs[0], -4.0, 4.0, (KERNEL_COHORTS, KERNEL_SPAN_TAPS), jnp.float32)
    quick_groups = jax.random.bernoulli(forked_seed_pairs[1], quick_share, (KERNEL_COHORTS, 1))
    quick_rate = jnp.exp(jax.random.uniform(forked_seed_pairs[2], (KERNEL_COHORTS, 1), jnp.float32, jnp.log(1.0 / 50.0), jnp.log(1.0 / 30.0)))
    slow_rate = jax.random.uniform(forked_seed_pairs[3], (KERNEL_COHORTS, 1), jnp.float32, 0.2, 0.8) / KERNEL_SPAN_TAPS
    decay_rate = jnp.where(quick_groups, quick_rate, slow_rate)
    delay_offset_number = jnp.arange(KERNEL_SPAN_TAPS, dtype=jnp.float32)[None, :]
    spike_sequence = jax.random.randint(forked_seed_pairs[4], (KERNEL_COHORTS, 3), 1, KERNEL_SPAN_TAPS).astype(jnp.float32)
    fading_profile = jnp.exp(-decay_rate * delay_offset_number)
    fading_profile = fading_profile * jnp.where(delay_offset_number >= spike_sequence[:, 0:1], 0.7, 1.0)
    fading_profile = fading_profile * jnp.where(delay_offset_number >= spike_sequence[:, 1:2], 0.7, 1.0)
    fading_profile = fading_profile * jnp.where(delay_offset_number >= spike_sequence[:, 2:3], 0.7, 1.0)
    normalize_factor = jnp.sqrt(2.0 * decay_rate / (1.0 - jnp.exp(-2.0 * decay_rate * KERNEL_SPAN_TAPS)))
    return (amplitude * fading_profile * normalize_factor).astype(jnp.bfloat16)


def steps_of(stream_key, extent, shards, low, top_value):
    def one(dim, blocks):
        draws = jax.random.uniform(jax.random.fold_in(jax.random.fold_in(stream_key, 6), dim), (blocks,), jnp.float32, low / len(shards), top_value / len(shards))
        return jnp.repeat(jnp.exp(draws), extent[dim] // blocks).reshape((-1,) + (1,) * (len(extent) - dim - 1))

    factor_of = one(*shards[0])
    for cut in shards[1:]:
        factor_of = factor_of * one(*cut)
    return factor_of


def centred(key, shape, scale, most, cuts=(), kind=jnp.bfloat16):
    entries = scale * jax.random.normal(key, shape, jnp.float32)
    if cuts:
        entries = entries * steps_of(key, shape, cuts, -0.22, 0.18)
    return jnp.clip(entries, -most, most).astype(kind)


def setup_inputs(seed: int = 0) -> dict:
    keys = jax.random.split(jax.random.key(seed), 6)
    gate_input = centred(keys[0], (TOKENS, D), 1.0, 6.0, ((0, 8), (1, 4)))
    key_input = centred(keys[1], (TOKENS, D), 1.0, 6.0, ((0, 8), (1, 4)))
    value_input = centred(keys[2], (TOKENS, D), 1.0, 6.0, ((0, 8), (1, 4)))
    filter_taps = draw_filter_taps(jax.random.fold_in(keys[5], 71), 0)
    out_weight = centred(keys[4], (OUT, D), D ** -0.5, 0.0625, ((1, 4),))
    return dict(gate_input=gate_input, key_input=key_input, value_input=value_input, filter_taps=filter_taps, out_weight=out_weight)


def causal_conv(signal, taps):
    length = signal.shape[-1]
    padded = length + taps.shape[-1]
    spectrum = jnp.fft.rfft(signal, n=padded, axis=-1) * jnp.fft.rfft(taps, n=padded, axis=-1)[:, None, :]
    return jnp.fft.irfft(spectrum, n=padded, axis=-1)[..., :length]


def smoothed_samples(operands):
    return causal_conv(operands[0], operands[1])


def reference(gate_input, key_input, value_input, filter_taps, out_weight):
    product = (key_input.astype(jnp.float32) * value_input.astype(jnp.float32)).astype(jnp.bfloat16)
    length = product.shape[0]
    signal = product.astype(jnp.float32).reshape(length, KERNEL_COHORTS, GROUP_SIZE).transpose(1, 2, 0)
    taps = filter_taps.astype(jnp.float32)
    batches = math.gcd(KERNEL_COHORTS, 8)
    conv = lax.map(smoothed_samples, (signal.reshape(batches, KERNEL_COHORTS // batches, GROUP_SIZE, length),
                                taps.reshape(batches, KERNEL_COHORTS // batches, KERNEL_SPAN_TAPS)))
    conv = conv.reshape(KERNEL_COHORTS, GROUP_SIZE, length).transpose(2, 0, 1).reshape(length, D)
    gated = (gate_input.astype(jnp.float32) * conv).astype(jnp.bfloat16)
    share = D // N_TP
    weight_parts = out_weight.reshape(OUT, N_TP, share).transpose(1, 0, 2)
    gated_parts = gated.reshape(length, N_TP, share).transpose(1, 0, 2)

    def accumulate(total, operands):
        partial_value = jnp.dot(operands[0], operands[1].T, preferred_element_type=jnp.float32)
        rounded = lax.optimization_barrier(partial_value.astype(jnp.bfloat16))
        return total + rounded.astype(jnp.float32), None

    total = lax.scan(accumulate, jnp.zeros((OUT, length), jnp.float32), (weight_parts, gated_parts))[0]
    return total.astype(jnp.bfloat16)
```

```python
import functools

import jax
import jax.numpy as jnp
from jax import lax
from jax.experimental import pallas as pl
from jax.experimental.pallas import tpu as pltpu
from jax.sharding import PartitionSpec as P

GROUP_SIZE = 16
LANES = 128
BLOCK = 256
CHUNKS = 4
UNROLL = 4
PASSES = 4
MESH = pl.DeviceIdType.MESH
BF16 = jnp.bfloat16
F32 = jnp.float32


def at(start, size, multiple=None):
    return pl.ds(pl.multiple_of(start, multiple or size), size)


def kernel(
    ranges,
    chips,
    gate,
    key,
    value,
    taps,
    weight,
    out,
    signal,
    other,
    gate_raw,
    mine,
    theirs,
    weights,
    part,
    landed,
    keys,
    values,
    taps_raw,
    lines,
    gate_t,
    kv_sem,
    local_sem,
    gate_sem,
    pair_send,
    pair_recv,
    halo_send,
    halo_recv,
    gated_send,
    gated_recv,
    up_send,
    up_recv,
    down_send,
    down_recv,
    out_sem,
):
    tokens, width = gate.shape
    half = width // 2
    piece = tokens // 2
    chunk = half // CHUNKS
    length = taps.shape[1]
    groups = half // GROUP_SIZE
    rows = weight.shape[0] // ranges
    tile_rows = rows // 2
    place = lax.axis_index("seq")
    z = lax.axis_index("tp")
    chip = place // 2
    core = place % 2
    sibling = (chip * 2 + 1 - core, z)
    last_range = ranges - 1
    has_next = chip < chips - 1
    has_previous = chip > 0
    own_column = 2 * tokens + core * tokens

    def load(ref, buffer, which, side, j):
        column = jnp.where(side == 0, core, 1 - core) * half + j * chunk
        return pltpu.make_async_copy(
            ref.at[:, at(column, chunk)], buffer.at[side], kv_sem.at[which, side]
        )

    def gate_local():
        return pltpu.make_async_copy(
            gate.at[:, at(core * half, half)],
            gate_raw.at[at(core * tokens, tokens)],
            local_sem.at[0],
        )

    def gate_remote():
        return pltpu.make_async_remote_copy(
            src_ref=gate.at[:, at((1 - core) * half, half)],
            dst_ref=gate_raw.at[at(core * tokens, tokens)],
            send_sem=gate_sem.at[0],
            recv_sem=gate_sem.at[1],
            device_id=sibling,
            device_id_type=MESH,
        )

    def taps_local():
        return pltpu.make_async_copy(
            taps.at[at(core * groups, groups)], taps_raw, local_sem.at[1]
        )

    def weight_local(side):
        column = (core if side == 0 else 1 - core) * half
        return pltpu.make_async_copy(
            weight.at[:, at(column, half)], weights.at[side], local_sem.at[2 + side]
        )

    def pair_copy(j):
        return pltpu.make_async_remote_copy(
            src_ref=other.at[at(j * chunk, chunk)],
            dst_ref=signal.at[at(j * chunk, chunk), at(own_column, tokens)],
            send_sem=pair_send.at[j],
            recv_sem=pair_recv.at[j],
            device_id=sibling,
            device_id_type=MESH,
        )

    def halo_copy(side, late, j):
        target = (chip + 1) * 2 + (core if side == 0 else 1 - core)
        if side == 0:
            source = signal.at[at(j * chunk, chunk), at(own_column + late * piece, piece)]
        else:
            source = other.at[at(j * chunk, chunk), late * piece : (late + 1) * piece]
        return pltpu.make_async_remote_copy(
            src_ref=source,
            dst_ref=signal.at[at(j * chunk, chunk), at(core * tokens + late * piece, piece)],
            send_sem=halo_send.at[side, late, j],
            recv_sem=halo_recv.at[core, late, j],
            device_id=(target, z),
            device_id_type=MESH,
        )

    def halo_wait(source_core, late, j):
        start = source_core * tokens + late * piece
        there = signal.at[at(j * chunk, chunk), start : start + piece]
        pltpu.make_async_remote_copy(
            src_ref=there,
            dst_ref=there,
            send_sem=halo_send.at[0, late, j],
            recv_sem=halo_recv.at[source_core, late, j],
            device_id=sibling,
            device_id_type=MESH,
        ).wait_recv()

    def gated_copy(q, j, first):
        column = tokens - (q + 1) * piece
        return pltpu.make_async_remote_copy(
            src_ref=mine.at[at(j * chunk, chunk), first : first + piece],
            dst_ref=theirs.at[at(j * chunk, chunk), column : column + piece],
            send_sem=gated_send.at[q, j],
            recv_sem=gated_recv.at[q, j],
            device_id=sibling,
            device_id_type=MESH,
        )

    def part_at(q, owner, m):
        return part.at[q, at(owner * rows + m * tile_rows, tile_rows)]

    def up_copy(q, owner, m):
        return pltpu.make_async_remote_copy(
            src_ref=part_at(q, owner, m),
            dst_ref=landed.at[q, owner, at(m * tile_rows, tile_rows)],
            send_sem=up_send.at[q, owner, m],
            recv_sem=up_recv.at[q, owner, m],
            device_id=(place, z + 1),
            device_id_type=MESH,
        )

    def down_slot(owner, receiver):
        return jnp.where(owner == receiver, ranges, owner)

    def down_copy(q, owner, m, receiver):
        return pltpu.make_async_remote_copy(
            src_ref=part_at(q, owner, m),
            dst_ref=landed.at[q, down_slot(owner, receiver), at(m * tile_rows, tile_rows)],
            send_sem=down_send.at[q, owner, m],
            recv_sem=down_recv.at[q, owner, m],
            device_id=(place, z - 1),
            device_id_type=MESH,
        )

    def out_copy(q, m):
        column = tokens - (q + 1) * piece
        return pltpu.make_async_copy(
            part_at(q, z, m),
            out.at[at(m * tile_rows, tile_rows), column : column + piece],
            out_sem.at[q, m],
        )

    def arrived(q, slot, m):
        return landed[q, slot, at(m * tile_rows, tile_rows)].astype(F32)

    def mine_of(q, owner, m):
        return part[q, at(owner * rows + m * tile_rows, tile_rows)].astype(F32)

    def put(q, owner, m, total):
        part[q, at(owner * rows + m * tile_rows, tile_rows)] = total.astype(BF16)

    def forward(q, item):
        m = item % 2
        upper = last_range - item // 2
        lower = item // 2

        @pl.when((z > 0) & (z < upper))
        def _():
            up_copy(q, upper, m).wait_recv()
            put(q, upper, m, mine_of(q, upper, m) + arrived(q, upper, m))
            up_copy(q, upper, m).start()

        @pl.when((z < last_range) & (z > lower))
        def _():
            down_copy(q, lower, m, z).wait_recv()
            put(q, lower, m, mine_of(q, lower, m) + arrived(q, lower, m))
            down_copy(q, lower, m, z - 1).start()

    items = 2 * (ranges - 2)

    def forward_slot(q, slot):
        first, count = slot * items // CHUNKS, (slot + 1) * items // CHUNKS - slot * items // CHUNKS

        def one(i, carry):
            forward(q, i)
            return carry

        lax.fori_loop(first, first + count, one, 0)

    def finish(q):
        def one(m, carry):
            @pl.when(z > 0)
            def _():
                up_copy(q, z, m).wait_recv()

            @pl.when(z < last_range)
            def _():
                down_copy(q, z, m, z).wait_recv()

            @pl.when(z == 0)
            def _():
                put(q, z, m, mine_of(q, z, m) + arrived(q, ranges, m))

            @pl.when((z > 0) & (z < last_range))
            def _():
                put(q, z, m, mine_of(q, z, m) + arrived(q, z, m) + arrived(q, ranges, m))

            @pl.when(z == last_range)
            def _():
                put(q, z, m, mine_of(q, z, m) + arrived(q, z, m))

            out_copy(q, m).start()
            return carry

        lax.fori_loop(0, 2, one, 0)

    barrier = pltpu.get_barrier_semaphore()

    def greet(device):
        pl.semaphore_signal(barrier, inc=1, device_id=device, device_id_type=MESH)

    for side in range(2):
        load(key, keys, 0, side, 0).start()
        load(value, values, 1, side, 0).start()
    taps_local().start()
    greet(sibling)

    @pl.when(has_previous)
    def _():
        greet((place - 2, z))
        greet((chip * 2 - 1 - core, z))

    @pl.when(has_next)
    def _():
        greet((place + 2, z))
        greet((chip * 2 + 3 - core, z))

    @pl.when(z > 0)
    def _():
        greet((place, z - 1))

    @pl.when(z < last_range)
    def _():
        greet((place, z + 1))

    one = lambda flag: jnp.where(flag, 1, 0)
    peers = 1 + 2 * one(has_previous) + 2 * one(has_next) + one(z > 0) + one(z < last_range)
    pl.semaphore_wait(barrier, peers)

    def product_chunk(j, carry):
        for side in range(2):
            load(key, keys, 0, side, j).wait()
            load(value, values, 1, side, j).wait()
            for block in range(tokens // BLOCK):
                span = slice(block * BLOCK, (block + 1) * BLOCK)
                product = keys[side, span].astype(F32) * values[side, span].astype(F32)
                turned = product.T.astype(BF16)
                if side == 0:
                    signal[at(j * chunk, chunk), at(own_column + block * BLOCK, BLOCK)] = turned
                else:
                    other[at(j * chunk, chunk), span] = turned

            @pl.when(j + 1 < CHUNKS)
            def _():
                load(key, keys, 0, side, j + 1).start()
                load(value, values, 1, side, j + 1).start()

            if side == 1:
                pair_copy(j).start()

            @pl.when(has_next & (core == 1))
            def _():
                halo_copy(side, 1, j).start()

        @pl.when(j == 0)
        def _():
            gate_local().start()
            gate_remote().start()

        return carry

    lax.fori_loop(0, CHUNKS, product_chunk, 0)
    weight_local(0).start()
    weight_local(1).start()
    taps_local().wait()
    lines[:, :length] = taps_raw[...].astype(F32)
    lines[:, length:] = jnp.zeros((groups, LANES), F32)

    @pl.when(jnp.logical_not(has_previous))
    def _():
        signal[:, : 2 * tokens] = jnp.zeros((half, 2 * tokens), BF16)

    per_block = BLOCK // LANES
    lag_tiles = length // LANES
    lag_blocks = lag_tiles + per_block
    blocks = piece // BLOCK

    def convolve(p, j):
        first = 2 * tokens - (p + 1) * piece
        window = 2 * tokens + first - length
        empty = jnp.zeros((LANES, LANES), BF16)

        def one_group(local):
            group = j * (chunk // GROUP_SIZE) + local
            here = at(group * GROUP_SIZE, GROUP_SIZE)
            left = jnp.concatenate(
                [
                    jnp.concatenate(
                        [
                            signal[
                                here,
                                window + block * BLOCK + lag * LANES : window
                                + block * BLOCK
                                + (lag + 1) * LANES,
                            ]
                            for block in range(blocks)
                        ],
                        axis=0,
                    )
                    for lag in range(lag_blocks)
                ],
                axis=1,
            )
            line = lines[pl.ds(group, 1), :]
            spread = jnp.broadcast_to(line, (LANES, line.shape[1]))
            band = pltpu.roll(spread, 0, 1, stride=1, stride_axis=0).astype(BF16)

            def tile(index):
                if index < 0 or index > lag_tiles:
                    return empty
                return band[:, index * LANES : (index + 1) * LANES]

            matrix = jnp.concatenate(
                [
                    jnp.concatenate(
                        [tile(lag_tiles + across - lag) for across in range(per_block)], axis=1
                    )
                    for lag in range(lag_blocks)
                ],
                axis=0,
            )
            conv = jnp.dot(left, matrix, preferred_element_type=F32)
            local_rows = at(local * GROUP_SIZE, GROUP_SIZE)
            for block in range(blocks):
                columns = slice(block * BLOCK, (block + 1) * BLOCK)
                result = gate_t[local_rows, columns] * conv[
                    block * GROUP_SIZE : (block + 1) * GROUP_SIZE
                ]
                mine[here, first + block * BLOCK : first + (block + 1) * BLOCK] = result.astype(BF16)

        def some(step, carry):
            for i in range(UNROLL):
                one_group(step * UNROLL + i)
            return carry

        lax.fori_loop(0, chunk // GROUP_SIZE // UNROLL, some, 0)

    def turn_gate(p, j):
        first = 2 * tokens - (p + 1) * piece
        gate_t[...] = gate_raw[first : first + piece, at(j * chunk, chunk)].astype(F32).T

    def project(p):
        q = p % 2
        first = 2 * tokens - (p + 1) * piece
        column = tokens - (q + 1) * piece

        def one(i, carry):
            step, m = i // 2, i % 2
            owner = jnp.where(2 * z < ranges, last_range - step, step)
            start = at(owner * rows + m * tile_rows, tile_rows)
            total = jnp.dot(
                weights[0, start], mine[:, first : first + piece], preferred_element_type=F32
            ) + jnp.dot(
                weights[1, start], theirs[:, column : column + piece], preferred_element_type=F32
            )
            part[q, start] = total.astype(BF16)

            @pl.when((z == 0) & (owner > 0))
            def _():
                up_copy(q, owner, m).start()

            @pl.when((z == last_range) & (owner < last_range))
            def _():
                down_copy(q, owner, m, z - 1).start()

            return carry

        lax.fori_loop(0, 2 * ranges, one, 0)

    for p in range(PASSES):
        owner_core = 1 if p < 2 else 0
        q = p % 2
        first = 2 * tokens - (p + 1) * piece

        def conv_chunk(j, carry, p=p, owner_core=owner_core, q=q, first=first):
            if p == 0:

                @pl.when(j == 0)
                def _():
                    gate_local().wait()
                    gate_remote().wait_recv()

            turn_gate(p, j)
            if p == 0:
                pair_copy(j).wait_recv()

            @pl.when(has_previous)
            def _():
                halo_wait(owner_core, 1 - q, j)

            if p < PASSES - 1:

                @pl.when((j == CHUNKS - 1) & has_next & (core == (1 if p < 1 else 0)))
                def _():
                    def one(i, inner):
                        for side in range(2):
                            halo_copy(side, 1 - (p + 1) % 2, i).start()
                        return inner

                    lax.fori_loop(0, CHUNKS, one, 0)

            if p in (2, 3):

                @pl.when((j == 0) & (core == 1))
                def _():
                    finish(p - 2)

            if p in (1, 2):

                @pl.when((j > 0) & (core == 1))
                def _():
                    forward_slot(p - 1, j - 1)

            if p == 3:

                @pl.when((j > 0) & (core == 0))
                def _():
                    forward_slot(0, j - 1)

            convolve(p, j)

            @pl.when(core != owner_core)
            def _():
                gated_copy(q, j, first).start()

            return carry

        lax.fori_loop(0, CHUNKS, conv_chunk, 0)
        if p in (1, 2):

            @pl.when(core == 1)
            def _(p=p):
                forward_slot(p - 1, CHUNKS - 1)

        if p == 3:

            @pl.when(core == 0)
            def _():
                forward_slot(0, CHUNKS - 1)

        if p == 0:
            weight_local(0).wait()
            weight_local(1).wait()

        @pl.when(core == owner_core)
        def _(p=p, q=q, first=first):
            def one(j, carry):
                gated_copy(q, j, first).wait_recv()
                return carry

            lax.fori_loop(0, CHUNKS, one, 0)
            project(p)

    @pl.when(core == 0)
    def _():
        finish(0)
        for slot in range(CHUNKS):
            forward_slot(1, slot)
        finish(1)

    gate_remote().wait_send()

    def pairs_done(j, carry):
        pair_copy(j).wait_send()
        for q in range(2):
            gated_copy(q, j, 0).wait_send()

        @pl.when(has_next)
        def _():
            for late in range(2):
                for side in range(2):
                    halo_copy(side, late, j).wait_send()

        return carry

    lax.fori_loop(0, CHUNKS, pairs_done, 0)

    def sums_done(i, carry):
        owner, m = i // 2, i % 2
        for q in range(2):

            @pl.when(owner > z)
            def _():
                up_copy(q, owner, m).wait_send()

            @pl.when(owner < z)
            def _():
                down_copy(q, owner, m, z - 1).wait_send()

        return carry

    lax.fori_loop(0, 2 * ranges, sums_done, 0)
    for q in range(2):
        for m in range(2):
            out_copy(q, m).wait()


def solution(mesh):
    ranges = mesh.shape["tp"]
    chips = mesh.shape["seq"] // 2

    def body(gate_input, key_input, value_input, filter_taps, out_weight):
        tokens, width = gate_input.shape
        half = width // 2
        chunk = half // CHUNKS
        piece = tokens // 2
        length = filter_taps.shape[1]
        outputs = out_weight.shape[0]
        rows = outputs // ranges
        groups = half // GROUP_SIZE
        dma = pltpu.SemaphoreType.DMA
        return pl.pallas_call(
            functools.partial(kernel, ranges, chips),
            in_specs=[pl.BlockSpec(memory_space=pl.ANY)] * 5,
            out_specs=pl.BlockSpec(memory_space=pl.ANY),
            out_shape=jax.ShapeDtypeStruct((rows, tokens), BF16),
            scratch_shapes=[
                pltpu.VMEM((half, 4 * tokens), BF16),
                pltpu.VMEM((half, tokens), BF16),
                pltpu.VMEM((2 * tokens, half), BF16),
                pltpu.VMEM((half, 2 * tokens), BF16),
                pltpu.VMEM((half, tokens), BF16),
                pltpu.VMEM((2, outputs, half), BF16),
                pltpu.VMEM((2, outputs, piece), BF16),
                pltpu.VMEM((2, ranges + 1, rows, piece), BF16),
                pltpu.VMEM((2, tokens, chunk), BF16),
                pltpu.VMEM((2, tokens, chunk), BF16),
                pltpu.VMEM((groups, length), BF16),
                pltpu.VMEM((groups, length + LANES), F32),
                pltpu.VMEM((chunk, piece), F32),
                dma((2, 2)),
                dma((4,)),
                dma((2,)),
                dma((CHUNKS,)),
                dma((CHUNKS,)),
                dma((2, 2, CHUNKS)),
                dma((2, 2, CHUNKS)),
                dma((2, CHUNKS)),
                dma((2, CHUNKS)),
                dma((2, ranges, 2)),
                dma((2, ranges, 2)),
                dma((2, ranges, 2)),
                dma((2, ranges, 2)),
                dma((2, 2)),
            ],
            compiler_params=pltpu.CompilerParams(
                collective_id=0, has_side_effects=True, vmem_limit_bytes=62 * 1024 * 1024
            ),
            cost_estimate=pl.CostEstimate(
                flops=2 * tokens * width * (length + outputs),
                bytes_accessed=2 * (3 * tokens * width + outputs * width + rows * tokens),
                transcendentals=0,
            ),
        )(gate_input, key_input, value_input, filter_taps, out_weight)

    return jax.shard_map(
        body,
        mesh=mesh,
        in_specs=(P("seq", "tp"), P("seq", "tp"), P("seq", "tp"), P("tp", None), P(None, "tp")),
        out_specs=P("tp", "seq"),
        check_vma=False,
    )
```

```python
import functools

import jax
import jax.numpy as jnp
from jax import lax
from jax.experimental import pallas as pl
from jax.experimental.pallas import tpu as pltpu
from jax.sharding import PartitionSpec as P

GROUP_SIZE = 16
LANES = 128
BLOCK = 256
CHUNKS = 4
UNROLL = 4
PASSES = 4
MESH = pl.DeviceIdType.MESH
BF16 = jnp.bfloat16
F32 = jnp.float32


def at(start, size, multiple=None):
    return pl.ds(pl.multiple_of(start, multiple or size), size)


def kernel(
    ranges,
    chips,
    gate,
    key,
    value,
    taps,
    weight,
    out,
    signal,
    other,
    gate_raw,
    mine,
    theirs,
    weights,
    part,
    landed,
    keys,
    values,
    taps_raw,
    lines,
    gate_t,
    kv_sem,
    local_sem,
    gate_sem,
    pair_send,
    pair_recv,
    halo_send,
    halo_recv,
    gated_send,
    gated_recv,
    up_send,
    up_recv,
    down_send,
    down_recv,
    out_sem,
):
    tokens, width = gate.shape
    half = width // 2
    piece = tokens // 2
    chunk = half // CHUNKS
    length = taps.shape[1]
    groups = half // GROUP_SIZE
    rows = weight.shape[0] // ranges
    tile_rows = rows // 2
    place = lax.axis_index("seq")
    z = lax.axis_index("tp")
    chip = place // 2
    core = place % 2
    sibling = (chip * 2 + 1 - core, z)
    last_range = ranges - 1
    has_next = chip < chips - 1
    has_previous = chip > 0
    own_column = 2 * tokens + core * tokens

    def load(ref, buffer, which, side, j):
        column = jnp.where(side == 0, core, 1 - core) * half + j * chunk
        return pltpu.make_async_copy(
            ref.at[:, at(column, chunk)], buffer.at[side], kv_sem.at[which, side]
        )

    def gate_local():
        return pltpu.make_async_copy(
            gate.at[:, at(core * half, half)],
            gate_raw.at[at(core * tokens, tokens)],
            local_sem.at[0],
        )

    def gate_remote():
        return pltpu.make_async_remote_copy(
            src_ref=gate.at[:, at((1 - core) * half, half)],
            dst_ref=gate_raw.at[at(core * tokens, tokens)],
            send_sem=gate_sem.at[0],
            recv_sem=gate_sem.at[1],
            device_id=sibling,
            device_id_type=MESH,
        )

    def taps_local():
        return pltpu.make_async_copy(
            taps.at[at(core * groups, groups)], taps_raw, local_sem.at[1]
        )

    def weight_local(side):
        column = (core if side == 0 else 1 - core) * half
        return pltpu.make_async_copy(
            weight.at[:, at(column, half)], weights.at[side], local_sem.at[2 + side]
        )

    def pair_copy(j):
        return pltpu.make_async_remote_copy(
            src_ref=other.at[at(j * chunk, chunk)],
            dst_ref=signal.at[at(j * chunk, chunk), at(own_column, tokens)],
            send_sem=pair_send.at[j],
            recv_sem=pair_recv.at[j],
            device_id=sibling,
            device_id_type=MESH,
        )

    def halo_copy(side, late, j):
        target = (chip + 1) * 2 + (core if side == 0 else 1 - core)
        if side == 0:
            source = signal.at[at(j * chunk, chunk), at(own_column + late * piece, piece)]
        else:
            source = other.at[at(j * chunk, chunk), late * piece : (late + 1) * piece]
        return pltpu.make_async_remote_copy(
            src_ref=source,
            dst_ref=signal.at[at(j * chunk, chunk), at(core * tokens + late * piece, piece)],
            send_sem=halo_send.at[side, late, j],
            recv_sem=halo_recv.at[core, late, j],
            device_id=(target, z),
            device_id_type=MESH,
        )

    def halo_wait(source_core, late, j):
        start = source_core * tokens + late * piece
        there = signal.at[at(j * chunk, chunk), start : start + piece]
        pltpu.make_async_remote_copy(
            src_ref=there,
            dst_ref=there,
            send_sem=halo_send.at[0, late, j],
            recv_sem=halo_recv.at[source_core, late, j],
            device_id=sibling,
            device_id_type=MESH,
        ).wait_recv()

    def gated_copy(q, j, first):
        column = tokens - (q + 1) * piece
        return pltpu.make_async_remote_copy(
            src_ref=mine.at[at(j * chunk, chunk), first : first + piece],
            dst_ref=theirs.at[at(j * chunk, chunk), column : column + piece],
            send_sem=gated_send.at[q, j],
            recv_sem=gated_recv.at[q, j],
            device_id=sibling,
            device_id_type=MESH,
        )

    def part_at(q, owner, m):
        return part.at[q, at(owner * rows + m * tile_rows, tile_rows)]

    def up_copy(q, owner, m):
        return pltpu.make_async_remote_copy(
            src_ref=part_at(q, owner, m),
            dst_ref=landed.at[q, owner, at(m * tile_rows, tile_rows)],
            send_sem=up_send.at[q, owner, m],
            recv_sem=up_recv.at[q, owner, m],
            device_id=(place, z + 1),
            device_id_type=MESH,
        )

    def down_slot(owner, receiver):
        return jnp.where(owner == receiver, ranges, owner)

    def down_copy(q, owner, m, receiver):
        return pltpu.make_async_remote_copy(
            src_ref=part_at(q, owner, m),
            dst_ref=landed.at[q, down_slot(owner, receiver), at(m * tile_rows, tile_rows)],
            send_sem=down_send.at[q, owner, m],
            recv_sem=down_recv.at[q, owner, m],
            device_id=(place, z - 1),
            device_id_type=MESH,
        )

    def out_copy(q, m):
        column = tokens - (q + 1) * piece
        return pltpu.make_async_copy(
            part_at(q, z, m),
            out.at[at(m * tile_rows, tile_rows), column : column + piece],
            out_sem.at[q, m],
        )

    def arrived(q, slot, m):
        return landed[q, slot, at(m * tile_rows, tile_rows)].astype(F32)

    def mine_of(q, owner, m):
        return part[q, at(owner * rows + m * tile_rows, tile_rows)].astype(F32)

    def put(q, owner, m, total):
        part[q, at(owner * rows + m * tile_rows, tile_rows)] = total.astype(BF16)

    def add(q, owner, m):
        put(q, owner, m, mine_of(q, owner, m) + arrived(q, owner, m))

    def forward(q, step):
        upper_item = jnp.maximum(step - 2 * z, 0)
        upper = last_range - upper_item // 2
        lower_item = jnp.maximum(step - 2 * (last_range - z), 0)
        lower = lower_item // 2

        @pl.when((step >= 2 * z) & (upper > z))
        def _():
            m = upper_item % 2

            @pl.when(z == 0)
            def _():
                up_copy(q, upper + 1, m).wait_send()

            @pl.when(z > 0)
            def _():
                up_copy(q, upper, m).wait_recv()
                add(q, upper, m)

            up_copy(q, upper, m).start()

        @pl.when((step >= 2 * (last_range - z)) & (lower < z))
        def _():
            m = lower_item % 2

            @pl.when(z == last_range)
            def _():
                down_copy(q, lower - 1, m, z - 1).wait_send()

            @pl.when(z < last_range)
            def _():
                down_copy(q, lower, m, z).wait_recv()
                add(q, lower, m)

            down_copy(q, lower, m, z - 1).start()

    items = 2 * (ranges - 2)

    def forward_slot(q, slot):
        def one(i, carry):
            forward(q, i + 2)
            return carry

        lax.fori_loop(slot * items // CHUNKS, (slot + 1) * items // CHUNKS, one, 0)

    def finish(q):
        def one(m, carry):
            @pl.when(z > 0)
            def _():
                up_copy(q, z, m).wait_recv()

            @pl.when(z < last_range)
            def _():
                down_copy(q, z, m, z).wait_recv()

            @pl.when(z == 0)
            def _():
                put(q, z, m, mine_of(q, z, m) + arrived(q, ranges, m))

            @pl.when((z > 0) & (z < last_range))
            def _():
                put(q, z, m, mine_of(q, z, m) + arrived(q, z, m) + arrived(q, ranges, m))

            @pl.when(z == last_range)
            def _():
                put(q, z, m, mine_of(q, z, m) + arrived(q, z, m))

            out_copy(q, m).start()
            return carry

        lax.fori_loop(0, 2, one, 0)

    barrier = pltpu.get_barrier_semaphore()

    def greet(device):
        pl.semaphore_signal(barrier, inc=1, device_id=device, device_id_type=MESH)

    for side in range(2):
        load(key, keys, 0, side, 0).start()
        load(value, values, 1, side, 0).start()
    taps_local().start()
    greet(sibling)

    @pl.when(has_previous)
    def _():
        greet((place - 2, z))
        greet((chip * 2 - 1 - core, z))

    @pl.when(has_next)
    def _():
        greet((place + 2, z))
        greet((chip * 2 + 3 - core, z))

    @pl.when(z > 0)
    def _():
        greet((place, z - 1))

    @pl.when(z < last_range)
    def _():
        greet((place, z + 1))

    one = lambda flag: jnp.where(flag, 1, 0)
    peers = 1 + 2 * one(has_previous) + 2 * one(has_next) + one(z > 0) + one(z < last_range)
    pl.semaphore_wait(barrier, peers)

    def product_chunk(j, carry):
        for side in range(2):
            load(key, keys, 0, side, j).wait()
            load(value, values, 1, side, j).wait()
            for block in range(tokens // BLOCK):
                span = slice(block * BLOCK, (block + 1) * BLOCK)
                product = keys[side, span].astype(F32) * values[side, span].astype(F32)
                turned = product.T.astype(BF16)
                if side == 0:
                    signal[at(j * chunk, chunk), at(own_column + block * BLOCK, BLOCK)] = turned
                else:
                    other[at(j * chunk, chunk), span] = turned

            @pl.when(j + 1 < CHUNKS)
            def _():
                load(key, keys, 0, side, j + 1).start()
                load(value, values, 1, side, j + 1).start()

            if side == 1:
                pair_copy(j).start()

            @pl.when(has_next & (core == 1))
            def _():
                halo_copy(side, 1, j).start()

        @pl.when(j == 0)
        def _():
            gate_local().start()
            gate_remote().start()

        return carry

    lax.fori_loop(0, CHUNKS, product_chunk, 0)
    weight_local(0).start()
    weight_local(1).start()
    taps_local().wait()
    lines[:, :length] = taps_raw[...].astype(F32)
    lines[:, length:] = jnp.zeros((groups, LANES), F32)

    @pl.when(jnp.logical_not(has_previous))
    def _():
        signal[:, : 2 * tokens] = jnp.zeros((half, 2 * tokens), BF16)

    per_block = BLOCK // LANES
    lag_tiles = length // LANES
    lag_blocks = lag_tiles + per_block
    blocks = piece // BLOCK

    def convolve(p, j):
        first = 2 * tokens - (p + 1) * piece
        window = 2 * tokens + first - length
        empty = jnp.zeros((LANES, LANES), BF16)

        def one_group(local):
            group = j * (chunk // GROUP_SIZE) + local
            here = at(group * GROUP_SIZE, GROUP_SIZE)
            left = jnp.concatenate(
                [
                    jnp.concatenate(
                        [
                            signal[
                                here,
                                window + block * BLOCK + lag * LANES : window
                                + block * BLOCK
                                + (lag + 1) * LANES,
                            ]
                            for block in range(blocks)
                        ],
                        axis=0,
                    )
                    for lag in range(lag_blocks)
                ],
                axis=1,
            )
            line = lines[pl.ds(group, 1), :]
            spread = jnp.broadcast_to(line, (LANES, line.shape[1]))
            band = pltpu.roll(spread, 0, 1, stride=1, stride_axis=0).astype(BF16)

            def tile(index):
                if index < 0 or index > lag_tiles:
                    return empty
                return band[:, index * LANES : (index + 1) * LANES]

            matrix = jnp.concatenate(
                [
                    jnp.concatenate(
                        [tile(lag_tiles + across - lag) for across in range(per_block)], axis=1
                    )
                    for lag in range(lag_blocks)
                ],
                axis=0,
            )
            conv = jnp.dot(left, matrix, preferred_element_type=F32)
            local_rows = at(local * GROUP_SIZE, GROUP_SIZE)
            for block in range(blocks):
                columns = slice(block * BLOCK, (block + 1) * BLOCK)
                result = gate_t[local_rows, columns] * conv[
                    block * GROUP_SIZE : (block + 1) * GROUP_SIZE
                ]
                mine[here, first + block * BLOCK : first + (block + 1) * BLOCK] = result.astype(BF16)

        def some(step, carry):
            for i in range(UNROLL):
                one_group(step * UNROLL + i)
            return carry

        lax.fori_loop(0, chunk // GROUP_SIZE // UNROLL, some, 0)

    def turn_gate(p, j):
        first = 2 * tokens - (p + 1) * piece
        gate_t[...] = gate_raw[first : first + piece, at(j * chunk, chunk)].astype(F32).T

    def project(p):
        q = p % 2
        first = 2 * tokens - (p + 1) * piece
        column = tokens - (q + 1) * piece

        def one(i, carry):
            step, m = i // 2, i % 2
            owner = jnp.where(2 * z < ranges, last_range - step, step)
            start = at(owner * rows + m * tile_rows, tile_rows)
            total = jnp.dot(
                weights[0, start], mine[:, first : first + piece], preferred_element_type=F32
            ) + jnp.dot(
                weights[1, start], theirs[:, column : column + piece], preferred_element_type=F32
            )
            part[q, start] = total.astype(BF16)

            @pl.when((z == 0) & (i < 2))
            def _():
                up_copy(q, owner, m).start()

            @pl.when((z == last_range) & (i < 2))
            def _():
                down_copy(q, owner, m, z - 1).start()

            return carry

        lax.fori_loop(0, 2 * ranges, one, 0)

    for p in range(PASSES):
        owner_core = 1 if p < 2 else 0
        q = p % 2
        first = 2 * tokens - (p + 1) * piece

        def conv_chunk(j, carry, p=p, owner_core=owner_core, q=q, first=first):
            if p == 0:

                @pl.when(j == 0)
                def _():
                    gate_local().wait()
                    gate_remote().wait_recv()

            turn_gate(p, j)
            if p == 0:
                pair_copy(j).wait_recv()

            @pl.when(has_previous)
            def _():
                halo_wait(owner_core, 1 - q, j)

            if p < PASSES - 1:

                @pl.when((j == CHUNKS - 1) & has_next & (core == (1 if p < 1 else 0)))
                def _():
                    def one(i, inner):
                        for side in range(2):
                            halo_copy(side, 1 - (p + 1) % 2, i).start()
                        return inner

                    lax.fori_loop(0, CHUNKS, one, 0)

            if p in (2, 3):

                @pl.when((j == 0) & (core == 1))
                def _():
                    finish(p - 2)

            if p in (1, 2):

                @pl.when(core == 1)
                def _():
                    forward_slot(p - 1, j)

            if p == 3:

                @pl.when(core == 0)
                def _():
                    forward_slot(0, j)

            convolve(p, j)

            @pl.when(core != owner_core)
            def _():
                gated_copy(q, j, first).start()

            return carry

        lax.fori_loop(0, CHUNKS, conv_chunk, 0)
        if p == 0:
            weight_local(0).wait()
            weight_local(1).wait()

        @pl.when(core == owner_core)
        def _(p=p, q=q, first=first):
            def one(j, carry):
                gated_copy(q, j, first).wait_recv()
                return carry

            lax.fori_loop(0, CHUNKS, one, 0)
            project(p)

    @pl.when(core == 0)
    def _():
        finish(0)
        lax.fori_loop(0, CHUNKS, lambda slot, carry: (forward_slot(1, slot), carry)[1], 0)
        finish(1)

    gate_remote().wait_send()

    def pairs_done(j, carry):
        pair_copy(j).wait_send()
        for q in range(2):
            gated_copy(q, j, 0).wait_send()

        @pl.when(has_next)
        def _():
            for late in range(2):
                for side in range(2):
                    halo_copy(side, late, j).wait_send()

        return carry

    lax.fori_loop(0, CHUNKS, pairs_done, 0)

    def sums_done(i, carry):
        owner, m = i // 2, i % 2
        for q in range(2):

            @pl.when((owner > z) & ((z > 0) | (owner == 1)))
            def _():
                up_copy(q, owner, m).wait_send()

            @pl.when((owner < z) & ((z < last_range) | (owner == last_range - 1)))
            def _():
                down_copy(q, owner, m, z - 1).wait_send()

        return carry

    lax.fori_loop(0, 2 * ranges, sums_done, 0)
    for q in range(2):
        for m in range(2):
            out_copy(q, m).wait()


def solution(mesh):
    ranges = mesh.shape["tp"]
    chips = mesh.shape["seq"] // 2

    def body(gate_input, key_input, value_input, filter_taps, out_weight):
        tokens, width = gate_input.shape
        half = width // 2
        chunk = half // CHUNKS
        piece = tokens // 2
        length = filter_taps.shape[1]
        outputs = out_weight.shape[0]
        rows = outputs // ranges
        groups = half // GROUP_SIZE
        dma = pltpu.SemaphoreType.DMA
        return pl.pallas_call(
            functools.partial(kernel, ranges, chips),
            in_specs=[pl.BlockSpec(memory_space=pl.ANY)] * 5,
            out_specs=pl.BlockSpec(memory_space=pl.ANY),
            out_shape=jax.ShapeDtypeStruct((rows, tokens), BF16),
            scratch_shapes=[
                pltpu.VMEM((half, 4 * tokens), BF16),
                pltpu.VMEM((half, tokens), BF16),
                pltpu.VMEM((2 * tokens, half), BF16),
                pltpu.VMEM((half, 2 * tokens), BF16),
                pltpu.VMEM((half, tokens), BF16),
                pltpu.VMEM((2, outputs, half), BF16),
                pltpu.VMEM((2, outputs, piece), BF16),
                pltpu.VMEM((2, ranges + 1, rows, piece), BF16),
                pltpu.VMEM((2, tokens, chunk), BF16),
                pltpu.VMEM((2, tokens, chunk), BF16),
                pltpu.VMEM((groups, length), BF16),
                pltpu.VMEM((groups, length + LANES), F32),
                pltpu.VMEM((chunk, piece), F32),
                dma((2, 2)),
                dma((4,)),
                dma((2,)),
                dma((CHUNKS,)),
                dma((CHUNKS,)),
                dma((2, 2, CHUNKS)),
                dma((2, 2, CHUNKS)),
                dma((2, CHUNKS)),
                dma((2, CHUNKS)),
                dma((2, ranges, 2)),
                dma((2, ranges, 2)),
                dma((2, ranges, 2)),
                dma((2, ranges, 2)),
                dma((2, 2)),
            ],
            compiler_params=pltpu.CompilerParams(
                collective_id=0, has_side_effects=True, vmem_limit_bytes=62 * 1024 * 1024
            ),
            cost_estimate=pl.CostEstimate(
                flops=2 * tokens * width * (length + outputs),
                bytes_accessed=2 * (3 * tokens * width + outputs * width + rows * tokens),
                transcendentals=0,
            ),
        )(gate_input, key_input, value_input, filter_taps, out_weight)

    return jax.shard_map(
        body,
        mesh=mesh,
        in_specs=(P("seq", "tp"), P("seq", "tp"), P("seq", "tp"), P("tp", None), P(None, "tp")),
        out_specs=P("tp", "seq"),
        check_vma=False,
    )
```

```python
import functools
import math

import jax
import jax.numpy as jnp
from jax import lax
from jax.experimental import pallas as pl
from jax.experimental.pallas import tpu as pltpu
from jax.sharding import PartitionSpec as P

GROUP_SIZE = 16
LANES = 128
BLOCK = 256
CONV_BLOCK = 128
CHUNKS = 4
UNROLL = 16
SHARES = (2, 3, 3, 4, 4)
MESH = pl.DeviceIdType.MESH
BF16 = jnp.bfloat16
F32 = jnp.float32


def at(start, size, multiple=None):
    return pl.ds(pl.multiple_of(start, multiple or size), size)


def kernel(
    ranges,
    chips,
    gate,
    key,
    value,
    taps,
    weight,
    out,
    signal,
    other,
    gate_raw,
    mine,
    theirs,
    weights,
    taps_raw,
    lines,
    gate_t,
    kv_sem,
    local_sem,
    gate_sem,
    pair_send,
    pair_recv,
    halo_send,
    halo_recv,
    gated_send,
    gated_recv,
    up_send,
    up_recv,
    down_send,
    down_recv,
    out_sem,
    pair_out_send,
    pair_out_recv,
    *sums,
):
    tokens, width = gate.shape
    half = width // 2
    passes = len(SHARES)
    parts, landeds = sums[:passes], sums[passes:]
    sizes = [2 * tokens * share // sum(SHARES) for share in SHARES]
    starts = [2 * tokens - sum(sizes[: p + 1]) for p in range(passes)]
    homes = [start // tokens for start in starts]
    chunk = half // CHUNKS
    length = taps.shape[1]
    groups = half // GROUP_SIZE
    rows = weight.shape[0] // ranges
    half_rows = rows // 2
    piece_rows = half_rows // 2
    place = lax.axis_index("seq")
    z = lax.axis_index("tp")
    chip = place // 2
    core = place % 2
    sibling = (chip * 2 + 1 - core, z)
    last_range = ranges - 1
    has_next = chip < chips - 1
    has_previous = chip > 0
    own_column = 2 * tokens + core * tokens

    def staged(which, side, j):
        return weights.at[which, at(j * tokens, tokens), side * chunk : (side + 1) * chunk]

    def load(which, side, j):
        column = (core if side == 0 else 1 - core) * half + j * chunk
        return pltpu.make_async_copy(
            (key, value)[which].at[:, at(column, chunk)],
            staged(which, side, j),
            kv_sem.at[which, side, j],
        )

    def gate_local():
        return pltpu.make_async_copy(
            gate.at[:, at(core * half, half)],
            gate_raw.at[at(core * tokens, tokens)],
            local_sem.at[0],
        )

    def gate_remote():
        return pltpu.make_async_remote_copy(
            src_ref=gate.at[:, at((1 - core) * half, half)],
            dst_ref=gate_raw.at[at(core * tokens, tokens)],
            send_sem=gate_sem.at[0],
            recv_sem=gate_sem.at[1],
            device_id=sibling,
            device_id_type=MESH,
        )

    def taps_local():
        return pltpu.make_async_copy(
            taps.at[at(core * groups, groups)], taps_raw, local_sem.at[1]
        )

    def weight_local(side):
        column = (core if side == 0 else 1 - core) * half
        return pltpu.make_async_copy(
            weight.at[:, at(column, half)], weights.at[side], local_sem.at[2 + side]
        )

    def pair_copy(j):
        return pltpu.make_async_remote_copy(
            src_ref=other.at[at(j * chunk, chunk)],
            dst_ref=signal.at[at(j * chunk, chunk), at(own_column, tokens)],
            send_sem=pair_send.at[j],
            recv_sem=pair_recv.at[j],
            device_id=sibling,
            device_id_type=MESH,
        )

    def halo_copy(side, p, j):
        target = (chip + 1) * 2 + (core if side == 0 else 1 - core)
        start, size = starts[p], sizes[p]
        here = at(j * chunk, chunk)
        if side == 0:
            source = signal.at[here, 2 * tokens + start : 2 * tokens + start + size]
        else:
            source = other.at[here, start % tokens : start % tokens + size]
        return pltpu.make_async_remote_copy(
            src_ref=source,
            dst_ref=signal.at[here, start : start + size],
            send_sem=halo_send.at[side, p, j],
            recv_sem=halo_recv.at[p, j],
            device_id=(target, z),
            device_id_type=MESH,
        )

    def gated_copy(p, j):
        here = (at(j * chunk, chunk), slice(starts[p], starts[p] + sizes[p]))
        return pltpu.make_async_remote_copy(
            src_ref=mine.at[here],
            dst_ref=theirs.at[here],
            send_sem=gated_send.at[p, j],
            recv_sem=gated_recv.at[p, j],
            device_id=sibling,
            device_id_type=MESH,
        )

    def spot(owner, m):
        return at(owner * half_rows + m * piece_rows, piece_rows)

    def part_at(p, owner, m):
        return parts[p].at[spot(owner, m)]

    def up_copy(q, owner, m):
        return pltpu.make_async_remote_copy(
            src_ref=part_at(q, owner, m),
            dst_ref=landeds[q].at[spot(owner, m)],
            send_sem=up_send.at[q, owner, m],
            recv_sem=up_recv.at[q, owner, m],
            device_id=(place, z + 1),
            device_id_type=MESH,
        )

    def down_slot(owner, receiver):
        return jnp.where(owner == receiver, ranges, owner)

    def down_copy(q, owner, m, receiver):
        return pltpu.make_async_remote_copy(
            src_ref=part_at(q, owner, m),
            dst_ref=landeds[q].at[spot(down_slot(owner, receiver), m)],
            send_sem=down_send.at[q, owner, m],
            recv_sem=down_recv.at[q, owner, m],
            device_id=(place, z - 1),
            device_id_type=MESH,
        )

    def out_at(p, writer, m):
        column = starts[p] % tokens
        return out.at[
            at(writer * half_rows + m * piece_rows, piece_rows), column : column + sizes[p]
        ]

    def out_copy(p, m):
        return pltpu.make_async_copy(part_at(p, z, m), out_at(p, core, m), out_sem.at[p, m])

    def pair_out_copy(p, m, writer):
        return pltpu.make_async_remote_copy(
            src_ref=part_at(p, z, m),
            dst_ref=out_at(p, writer, m),
            send_sem=pair_out_send.at[p, m],
            recv_sem=pair_out_recv.at[p, m],
            device_id=sibling,
            device_id_type=MESH,
        )

    def arrived(q, slot, m):
        return landeds[q][spot(slot, m)].astype(F32)

    def mine_of(q, owner, m):
        return parts[q][spot(owner, m)].astype(F32)

    def put(q, owner, m, total):
        parts[q][spot(owner, m)] = total.astype(BF16)

    def add(q, owner, m):
        put(q, owner, m, mine_of(q, owner, m) + arrived(q, owner, m))

    def forward(q, step):
        upper_item = jnp.maximum(step - 2 * z, 0)
        upper = last_range - upper_item // 2
        lower_item = jnp.maximum(step - 2 * (last_range - z), 0)
        lower = lower_item // 2

        @pl.when((step >= 2 * z) & (upper > z))
        def _():
            m = upper_item % 2

            @pl.when(z == 0)
            def _():
                up_copy(q, upper + 1, m).wait_send()

            @pl.when(z > 0)
            def _():
                up_copy(q, upper, m).wait_recv()
                add(q, upper, m)

            up_copy(q, upper, m).start()

        @pl.when((step >= 2 * (last_range - z)) & (lower < z))
        def _():
            m = lower_item % 2

            @pl.when(z == last_range)
            def _():
                down_copy(q, lower - 1, m, z - 1).wait_send()

            @pl.when(z < last_range)
            def _():
                down_copy(q, lower, m, z).wait_recv()
                add(q, lower, m)

            down_copy(q, lower, m, z - 1).start()

    items = 2 * (ranges - 2)

    def forward_slot(q, slot):
        def one(i, carry):
            forward(q, i + 2)
            return carry

        lax.fori_loop(slot * items // CHUNKS, (slot + 1) * items // CHUNKS, one, 0)

    def finish(q):
        def one(m, carry):
            @pl.when(z > 0)
            def _():
                up_copy(q, z, m).wait_recv()

            @pl.when(z < last_range)
            def _():
                down_copy(q, z, m, z).wait_recv()

            @pl.when(z == 0)
            def _():
                put(q, z, m, mine_of(q, z, m) + arrived(q, ranges, m))

            @pl.when((z > 0) & (z < last_range))
            def _():
                put(q, z, m, mine_of(q, z, m) + arrived(q, z, m) + arrived(q, ranges, m))

            @pl.when(z == last_range)
            def _():
                put(q, z, m, mine_of(q, z, m) + arrived(q, z, m))

            pl.when(core == homes[q])(lambda: out_copy(q, m).start())
            pl.when(core != homes[q])(lambda: pair_out_copy(q, m, core).start())
            return carry

        lax.fori_loop(0, 2, one, 0)

    barrier = pltpu.get_barrier_semaphore()

    def greet(device):
        pl.semaphore_signal(barrier, inc=1, device_id=device, device_id_type=MESH)

    for j in range(CHUNKS):
        for side in range(2):
            load(0, side, j).start()
            load(1, side, j).start()
    taps_local().start()
    greet(sibling)

    @pl.when(has_previous)
    def _():
        greet((place - 2, z))
        greet((chip * 2 - 1 - core, z))

    @pl.when(has_next)
    def _():
        greet((place + 2, z))
        greet((chip * 2 + 3 - core, z))

    @pl.when(z > 0)
    def _():
        greet((place, z - 1))

    @pl.when(z < last_range)
    def _():
        greet((place, z + 1))

    one = lambda flag: jnp.where(flag, 1, 0)
    peers = 1 + 2 * one(has_previous) + 2 * one(has_next) + one(z > 0) + one(z < last_range)
    pl.semaphore_wait(barrier, peers)

    def product_chunk(j, carry):
        for side in range(2):
            load(0, side, j).wait()
            load(1, side, j).wait()
            for block in range(tokens // BLOCK):
                span = slice(block * BLOCK, (block + 1) * BLOCK)
                here = at(j * tokens + block * BLOCK, BLOCK)
                column = slice(side * chunk, (side + 1) * chunk)
                product = weights[0, here, column].astype(F32) * weights[1, here, column].astype(F32)
                turned = product.T.astype(BF16)
                if side == 0:
                    signal[at(j * chunk, chunk), at(own_column + block * BLOCK, BLOCK)] = turned
                else:
                    other[at(j * chunk, chunk), span] = turned

            if side == 1:
                pair_copy(j).start()

            @pl.when(has_next & (core == 1))
            def _():
                halo_copy(side, 0, j).start()

        @pl.when(j == 0)
        def _():
            gate_local().start()
            gate_remote().start()

        return carry

    lax.fori_loop(0, CHUNKS, product_chunk, 0)
    weight_local(0).start()
    weight_local(1).start()
    taps_local().wait()
    lines[:, :length] = taps_raw[...].astype(F32)
    lines[:, length:] = jnp.zeros((groups, LANES), F32)

    @pl.when(jnp.logical_not(has_previous))
    def _():
        signal[:, : 2 * tokens] = jnp.zeros((half, 2 * tokens), BF16)

    per_block = CONV_BLOCK // LANES
    lag_tiles = length // LANES
    lag_blocks = lag_tiles + per_block

    def convolve(p, j):
        first = starts[p]
        blocks = sizes[p] // CONV_BLOCK
        window = 2 * tokens + first - length
        empty = jnp.zeros((LANES, LANES), BF16)

        def one_group(local):
            group = j * (chunk // GROUP_SIZE) + local
            here = at(group * GROUP_SIZE, GROUP_SIZE)
            left = jnp.concatenate(
                [
                    jnp.concatenate(
                        [
                            signal[
                                here,
                                window + block * CONV_BLOCK + lag * LANES : window
                                + block * CONV_BLOCK
                                + (lag + 1) * LANES,
                            ]
                            for block in range(blocks)
                        ],
                        axis=0,
                    )
                    for lag in range(lag_blocks)
                ],
                axis=1,
            )
            line = lines[pl.ds(group, 1), :]
            spread = jnp.broadcast_to(line, (LANES, line.shape[1]))
            band = pltpu.roll(spread, 0, 1, stride=1, stride_axis=0).astype(BF16)

            def tile(index):
                if index < 0 or index > lag_tiles:
                    return empty
                return band[:, index * LANES : (index + 1) * LANES]

            matrix = jnp.concatenate(
                [
                    jnp.concatenate(
                        [tile(lag_tiles + across - lag) for across in range(per_block)], axis=1
                    )
                    for lag in range(lag_blocks)
                ],
                axis=0,
            )
            conv = jnp.dot(left, matrix, preferred_element_type=F32)
            local_rows = at(local * GROUP_SIZE, GROUP_SIZE)
            for block in range(blocks):
                columns = slice(block * CONV_BLOCK, (block + 1) * CONV_BLOCK)
                result = gate_t[local_rows, columns] * conv[
                    block * GROUP_SIZE : (block + 1) * GROUP_SIZE
                ]
                mine[here, first + block * CONV_BLOCK : first + (block + 1) * CONV_BLOCK] = result.astype(BF16)

        unroll = math.gcd(chunk // GROUP_SIZE, UNROLL)

        def some(step, carry):
            for i in range(unroll):
                one_group(step * unroll + i)
            return carry

        lax.fori_loop(0, chunk // GROUP_SIZE // unroll, some, 0)

    def turn_gate(p, j):
        first, size = starts[p], sizes[p]
        gate_t[:, :size] = gate_raw[first : first + size, at(j * chunk, chunk)].astype(F32).T

    def project(p):
        columns = slice(starts[p], starts[p] + sizes[p])

        def one(i, carry):
            owner = jnp.where(2 * z < ranges, last_range - i, i)
            start = at(owner * rows + core * half_rows, half_rows)
            total = jnp.dot(
                weights[0, start], mine[:, columns], preferred_element_type=F32
            ) + jnp.dot(weights[1, start], theirs[:, columns], preferred_element_type=F32)
            parts[p][at(owner * half_rows, half_rows)] = total.astype(BF16)

            @pl.when((z == 0) & (i == 0))
            def _():
                for m in range(2):
                    up_copy(p, owner, m).start()

            @pl.when((z == last_range) & (i == 0))
            def _():
                for m in range(2):
                    down_copy(p, owner, m, z - 1).start()

            return carry

        lax.fori_loop(0, ranges, one, 0)

    def send_halo(p, chunks):
        @pl.when(has_next & (core == homes[p]))
        def _():
            def one(i, carry):
                for side in range(2):
                    halo_copy(side, p, i).start()
                return carry

            lax.fori_loop(*chunks, one, 0)

    for p in range(passes):

        def conv_chunk(j, carry, p=p):
            if p == 0:

                @pl.when(j == 0)
                def _():
                    gate_local().wait()
                    gate_remote().wait_recv()

            turn_gate(p, j)
            if p == 0:
                pair_copy(j).wait_recv()

            @pl.when(has_previous)
            def _():
                halo_copy(0, p, j).wait_recv()

            if p == 0:
                pl.when((j > 0) & (j < CHUNKS - 1))(lambda: send_halo(1, (j - 1, j)))
                pl.when(j == CHUNKS - 1)(lambda: send_halo(1, (j - 1, j + 1)))
            elif p == 1:
                send_halo(p + 1, (j, j + 1))
            elif p < passes - 1:
                pl.when(j == CHUNKS - 1)(lambda: send_halo(p + 1, (0, CHUNKS)))
            if p > 0:
                forward_slot(p - 1, j)
            if p > 1:
                pl.when(j == 0)(lambda: finish(p - 2))
            convolve(p, j)
            gated_copy(p, j).start()
            return carry

        lax.fori_loop(0, CHUNKS, conv_chunk, 0)
        if p == 0:
            weight_local(0).wait()
            weight_local(1).wait()

        def gated_here(j, carry, p=p):
            gated_copy(p, j).wait_recv()
            return carry

        lax.fori_loop(0, CHUNKS, gated_here, 0)
        project(p)

    def last_slots(slot, carry):
        forward_slot(passes - 1, slot)
        pl.when(slot == CHUNKS // 2 - 1)(lambda: finish(passes - 2))
        return carry

    lax.fori_loop(0, CHUNKS, last_slots, 0)
    finish(passes - 1)

    gate_remote().wait_send()

    def pairs_done(j, carry):
        pair_copy(j).wait_send()

        for p in range(passes):
            gated_copy(p, j).wait_send()

            @pl.when(has_next & (core == homes[p]))
            def _():
                for side in range(2):
                    halo_copy(side, p, j).wait_send()

        return carry

    lax.fori_loop(0, CHUNKS, pairs_done, 0)

    def sums_done(i, carry):
        owner, m = i // 2, i % 2
        for q in range(passes):

            @pl.when((owner > z) & ((z > 0) | (owner == 1)))
            def _():
                up_copy(q, owner, m).wait_send()

            @pl.when((owner < z) & ((z < last_range) | (owner == last_range - 1)))
            def _():
                down_copy(q, owner, m, z - 1).wait_send()

        return carry

    lax.fori_loop(0, 2 * ranges, sums_done, 0)
    for p in range(passes):
        for m in range(2):

            @pl.when(core == homes[p])
            def _():
                out_copy(p, m).wait()
                pair_out_copy(p, m, 1 - core).wait_recv()

            @pl.when(core != homes[p])
            def _():
                pair_out_copy(p, m, core).wait_send()


def solution(mesh):
    ranges = mesh.shape["tp"]
    chips = mesh.shape["seq"] // 2

    def body(gate_input, key_input, value_input, filter_taps, out_weight):
        tokens, width = gate_input.shape
        half = width // 2
        chunk = half // CHUNKS
        sizes = [2 * tokens * share // sum(SHARES) for share in SHARES]
        count = len(SHARES)
        length = filter_taps.shape[1]
        outputs = out_weight.shape[0]
        rows = outputs // ranges
        groups = half // GROUP_SIZE
        dma = pltpu.SemaphoreType.DMA
        return pl.pallas_call(
            functools.partial(kernel, ranges, chips),
            in_specs=[pl.BlockSpec(memory_space=pl.ANY)] * 5,
            out_specs=pl.BlockSpec(memory_space=pl.ANY),
            out_shape=jax.ShapeDtypeStruct((rows, tokens), BF16),
            scratch_shapes=[
                pltpu.VMEM((half, 4 * tokens), BF16),
                pltpu.VMEM((half, tokens), BF16),
                pltpu.VMEM((2 * tokens, half), BF16),
                pltpu.VMEM((half, 2 * tokens), BF16),
                pltpu.VMEM((half, 2 * tokens), BF16),
                pltpu.VMEM((2, outputs, half), BF16),
                pltpu.VMEM((groups, length), BF16),
                pltpu.VMEM((groups, length + LANES), F32),
                pltpu.VMEM((chunk, max(sizes)), F32),
                dma((2, 2, CHUNKS)),
                dma((4,)),
                dma((2,)),
                dma((CHUNKS,)),
                dma((CHUNKS,)),
                dma((2, count, CHUNKS)),
                *[dma((count, CHUNKS))] * 3,
                *[dma((count, ranges, 2))] * 4,
                *[dma((count, 2))] * 3,
                *[pltpu.VMEM((outputs // 2, size), BF16) for size in sizes],
                *[pltpu.VMEM(((ranges + 1) * rows // 2, size), BF16) for size in sizes],
            ],
            compiler_params=pltpu.CompilerParams(
                collective_id=0, has_side_effects=True, vmem_limit_bytes=62 * 1024 * 1024
            ),
            cost_estimate=pl.CostEstimate(
                flops=2 * tokens * width * (length + outputs),
                bytes_accessed=2 * (3 * tokens * width + outputs * width + rows * tokens),
                transcendentals=0,
            ),
        )(gate_input, key_input, value_input, filter_taps, out_weight)

    return jax.shard_map(
        body,
        mesh=mesh,
        in_specs=(P("seq", "tp"), P("seq", "tp"), P("seq", "tp"), P("tp", None), P(None, "tp")),
        out_specs=P("tp", "seq"),
        check_vma=False,
    )
```

```python
import functools
import math

import jax
import jax.numpy as jnp
from jax import lax
from jax.experimental import pallas as pl
from jax.experimental.pallas import tpu as pltpu
from jax.sharding import PartitionSpec as P

GROUP_SIZE = 16
LANES = 128
BLOCK = 256
CONV_BLOCK = 128
CHUNKS = 4
UNROLL = 16
SHARES = (2, 3, 3, 4, 4)
MESH = pl.DeviceIdType.MESH
BF16 = jnp.bfloat16
F32 = jnp.float32


def at(start, size, multiple=None):
    return pl.ds(pl.multiple_of(start, multiple or size), size)


def kernel(
    ranges,
    chips,
    gate,
    key,
    value,
    taps,
    weight,
    out,
    signal,
    other,
    gate_raw,
    mine,
    theirs,
    weights,
    taps_raw,
    lines,
    gate_t,
    kv_sem,
    local_sem,
    gate_sem,
    pair_send,
    pair_recv,
    halo_send,
    halo_recv,
    gated_send,
    gated_recv,
    up_send,
    up_recv,
    down_send,
    down_recv,
    out_sem,
    pair_out_send,
    pair_out_recv,
    *sums,
):
    tokens, width = gate.shape
    half = width // 2
    passes = len(SHARES)
    parts, landeds = sums[:passes], sums[passes:]
    sizes = [2 * tokens * share // sum(SHARES) for share in SHARES]
    starts = [2 * tokens - sum(sizes[: p + 1]) for p in range(passes)]
    homes = [start // tokens for start in starts]
    chunk = half // CHUNKS
    length = taps.shape[1]
    groups = half // GROUP_SIZE
    rows = weight.shape[0] // ranges
    half_rows = rows // 2
    piece_rows = half_rows // 2
    place = lax.axis_index("seq")
    z = lax.axis_index("tp")
    chip = place // 2
    core = place % 2
    sibling = (chip * 2 + 1 - core, z)
    last_range = ranges - 1
    has_next = chip < chips - 1
    has_previous = chip > 0
    own_column = 2 * tokens + core * tokens

    def staged(which, side, j):
        return weights.at[which, at(j * tokens, tokens), side * chunk : (side + 1) * chunk]

    def load(which, side, j):
        column = (core if side == 0 else 1 - core) * half + j * chunk
        return pltpu.make_async_copy(
            (key, value)[which].at[:, at(column, chunk)],
            staged(which, side, j),
            kv_sem.at[which, side, j],
        )

    def gate_rows(p):
        return (
            slice(starts[p] % tokens, starts[p] % tokens + sizes[p]),
            slice(starts[p], starts[p] + sizes[p]),
        )

    def gate_local(p):
        here, there = gate_rows(p)
        return pltpu.make_async_copy(
            gate.at[here, at(core * half, half)], gate_raw.at[there], gate_sem.at[0, p]
        )

    def gate_remote(p):
        here, there = gate_rows(p)
        return pltpu.make_async_remote_copy(
            src_ref=gate.at[here, at((1 - core) * half, half)],
            dst_ref=gate_raw.at[there],
            send_sem=gate_sem.at[1, p],
            recv_sem=gate_sem.at[2, p],
            device_id=sibling,
            device_id_type=MESH,
        )

    def send_gate(p):
        @pl.when(core == homes[p])
        def _():
            gate_local(p).start()
            gate_remote(p).start()

    def taps_local():
        return pltpu.make_async_copy(
            taps.at[at(core * groups, groups)], taps_raw, local_sem.at[1]
        )

    def weight_local(side):
        column = (core if side == 0 else 1 - core) * half
        return pltpu.make_async_copy(
            weight.at[:, at(column, half)], weights.at[side], local_sem.at[2 + side]
        )

    def pair_copy(j):
        return pltpu.make_async_remote_copy(
            src_ref=other.at[at(j * chunk, chunk)],
            dst_ref=signal.at[at(j * chunk, chunk), at(own_column, tokens)],
            send_sem=pair_send.at[j],
            recv_sem=pair_recv.at[j],
            device_id=sibling,
            device_id_type=MESH,
        )

    def halo_copy(side, p, j):
        target = (chip + 1) * 2 + (core if side == 0 else 1 - core)
        start, size = starts[p], sizes[p]
        here = at(j * chunk, chunk)
        if side == 0:
            source = signal.at[here, 2 * tokens + start : 2 * tokens + start + size]
        else:
            source = other.at[here, start % tokens : start % tokens + size]
        return pltpu.make_async_remote_copy(
            src_ref=source,
            dst_ref=signal.at[here, start : start + size],
            send_sem=halo_send.at[side, p, j],
            recv_sem=halo_recv.at[p, j],
            device_id=(target, z),
            device_id_type=MESH,
        )

    def gated_copy(p, j):
        here = (at(j * chunk, chunk), slice(starts[p], starts[p] + sizes[p]))
        return pltpu.make_async_remote_copy(
            src_ref=mine.at[here],
            dst_ref=theirs.at[here],
            send_sem=gated_send.at[p, j],
            recv_sem=gated_recv.at[p, j],
            device_id=sibling,
            device_id_type=MESH,
        )

    def spot(owner, m):
        return at(owner * half_rows + m * piece_rows, piece_rows)

    def part_at(p, owner, m):
        return parts[p].at[spot(owner, m)]

    def up_copy(q, owner, m):
        return pltpu.make_async_remote_copy(
            src_ref=part_at(q, owner, m),
            dst_ref=landeds[q].at[spot(owner, m)],
            send_sem=up_send.at[q, owner, m],
            recv_sem=up_recv.at[q, owner, m],
            device_id=(place, z + 1),
            device_id_type=MESH,
        )

    def down_slot(owner, receiver):
        return jnp.where(owner == receiver, ranges, owner)

    def down_copy(q, owner, m, receiver):
        return pltpu.make_async_remote_copy(
            src_ref=part_at(q, owner, m),
            dst_ref=landeds[q].at[spot(down_slot(owner, receiver), m)],
            send_sem=down_send.at[q, owner, m],
            recv_sem=down_recv.at[q, owner, m],
            device_id=(place, z - 1),
            device_id_type=MESH,
        )

    def out_at(p, writer, m):
        column = starts[p] % tokens
        return out.at[
            at(writer * half_rows + m * piece_rows, piece_rows), column : column + sizes[p]
        ]

    def out_copy(p, m):
        return pltpu.make_async_copy(part_at(p, z, m), out_at(p, core, m), out_sem.at[p, m])

    def pair_out_copy(p, m, writer):
        return pltpu.make_async_remote_copy(
            src_ref=part_at(p, z, m),
            dst_ref=out_at(p, writer, m),
            send_sem=pair_out_send.at[p, m],
            recv_sem=pair_out_recv.at[p, m],
            device_id=sibling,
            device_id_type=MESH,
        )

    def arrived(q, slot, m):
        return landeds[q][spot(slot, m)].astype(F32)

    def mine_of(q, owner, m):
        return parts[q][spot(owner, m)].astype(F32)

    def put(q, owner, m, total):
        parts[q][spot(owner, m)] = total.astype(BF16)

    def add(q, owner, m):
        put(q, owner, m, mine_of(q, owner, m) + arrived(q, owner, m))

    def forward(q, step):
        upper_item = jnp.maximum(step - 2 * z, 0)
        upper = last_range - upper_item // 2
        lower_item = jnp.maximum(step - 2 * (last_range - z), 0)
        lower = lower_item // 2

        @pl.when((step >= 2 * z) & (upper > z))
        def _():
            m = upper_item % 2

            @pl.when(z == 0)
            def _():
                up_copy(q, upper + 1, m).wait_send()

            @pl.when(z > 0)
            def _():
                up_copy(q, upper, m).wait_recv()
                add(q, upper, m)

            up_copy(q, upper, m).start()

        @pl.when((step >= 2 * (last_range - z)) & (lower < z))
        def _():
            m = lower_item % 2

            @pl.when(z == last_range)
            def _():
                down_copy(q, lower - 1, m, z - 1).wait_send()

            @pl.when(z < last_range)
            def _():
                down_copy(q, lower, m, z).wait_recv()
                add(q, lower, m)

            down_copy(q, lower, m, z - 1).start()

    items = 2 * (ranges - 2)

    def forward_slot(q, slot):
        def one(i, carry):
            forward(q, i + 2)
            return carry

        lax.fori_loop(slot * items // CHUNKS, (slot + 1) * items // CHUNKS, one, 0)

    def finish(q):
        def one(m, carry):
            @pl.when(z > 0)
            def _():
                up_copy(q, z, m).wait_recv()

            @pl.when(z < last_range)
            def _():
                down_copy(q, z, m, z).wait_recv()

            @pl.when(z == 0)
            def _():
                put(q, z, m, mine_of(q, z, m) + arrived(q, ranges, m))

            @pl.when((z > 0) & (z < last_range))
            def _():
                put(q, z, m, mine_of(q, z, m) + arrived(q, z, m) + arrived(q, ranges, m))

            @pl.when(z == last_range)
            def _():
                put(q, z, m, mine_of(q, z, m) + arrived(q, z, m))

            pl.when(core == homes[q])(lambda: out_copy(q, m).start())
            pl.when(core != homes[q])(lambda: pair_out_copy(q, m, core).start())
            return carry

        lax.fori_loop(0, 2, one, 0)

    barrier = pltpu.get_barrier_semaphore()

    def greet(device):
        pl.semaphore_signal(barrier, inc=1, device_id=device, device_id_type=MESH)

    for j in range(CHUNKS):
        for side in range(2):
            load(0, side, j).start()
            load(1, side, j).start()
    taps_local().start()
    greet(sibling)

    @pl.when(has_previous)
    def _():
        greet((place - 2, z))
        greet((chip * 2 - 1 - core, z))

    @pl.when(has_next)
    def _():
        greet((place + 2, z))
        greet((chip * 2 + 3 - core, z))

    @pl.when(z > 0)
    def _():
        greet((place, z - 1))

    @pl.when(z < last_range)
    def _():
        greet((place, z + 1))

    one = lambda flag: jnp.where(flag, 1, 0)
    peers = 1 + 2 * one(has_previous) + 2 * one(has_next) + one(z > 0) + one(z < last_range)
    pl.semaphore_wait(barrier, peers)

    def product_chunk(j, carry):
        for side in range(2):
            load(0, side, j).wait()
            load(1, side, j).wait()
            for block in range(tokens // BLOCK):
                span = slice(block * BLOCK, (block + 1) * BLOCK)
                here = at(j * tokens + block * BLOCK, BLOCK)
                column = slice(side * chunk, (side + 1) * chunk)
                product = weights[0, here, column].astype(F32) * weights[1, here, column].astype(F32)
                turned = product.T.astype(BF16)
                if side == 0:
                    signal[at(j * chunk, chunk), at(own_column + block * BLOCK, BLOCK)] = turned
                else:
                    other[at(j * chunk, chunk), span] = turned

            if side == 1:
                pair_copy(j).start()

            @pl.when(has_next & (core == 1))
            def _():
                halo_copy(side, 0, j).start()

        return carry

    send_gate(0)
    lax.fori_loop(0, CHUNKS, product_chunk, 0)
    send_gate(1)
    weight_local(0).start()
    weight_local(1).start()
    taps_local().wait()
    lines[:, :length] = taps_raw[...].astype(F32)
    lines[:, length:] = jnp.zeros((groups, LANES), F32)

    @pl.when(jnp.logical_not(has_previous))
    def _():
        signal[:, : 2 * tokens] = jnp.zeros((half, 2 * tokens), BF16)

    per_block = CONV_BLOCK // LANES
    lag_tiles = length // LANES
    lag_blocks = lag_tiles + per_block

    def convolve(p, j):
        first = starts[p]
        blocks = sizes[p] // CONV_BLOCK
        window = 2 * tokens + first - length
        empty = jnp.zeros((LANES, LANES), BF16)

        def one_group(local):
            group = j * (chunk // GROUP_SIZE) + local
            here = at(group * GROUP_SIZE, GROUP_SIZE)
            left = jnp.concatenate(
                [
                    jnp.concatenate(
                        [
                            signal[
                                here,
                                window + block * CONV_BLOCK + lag * LANES : window
                                + block * CONV_BLOCK
                                + (lag + 1) * LANES,
                            ]
                            for block in range(blocks)
                        ],
                        axis=0,
                    )
                    for lag in range(lag_blocks)
                ],
                axis=1,
            )
            line = lines[pl.ds(group, 1), :]
            spread = jnp.broadcast_to(line, (LANES, line.shape[1]))
            band = pltpu.roll(spread, 0, 1, stride=1, stride_axis=0).astype(BF16)

            def tile(index):
                if index < 0 or index > lag_tiles:
                    return empty
                return band[:, index * LANES : (index + 1) * LANES]

            matrix = jnp.concatenate(
                [
                    jnp.concatenate(
                        [tile(lag_tiles + across - lag) for across in range(per_block)], axis=1
                    )
                    for lag in range(lag_blocks)
                ],
                axis=0,
            )
            conv = jnp.dot(left, matrix, preferred_element_type=F32)
            local_rows = at(local * GROUP_SIZE, GROUP_SIZE)
            for block in range(blocks):
                columns = slice(block * CONV_BLOCK, (block + 1) * CONV_BLOCK)
                result = gate_t[local_rows, columns] * conv[
                    block * GROUP_SIZE : (block + 1) * GROUP_SIZE
                ]
                mine[here, first + block * CONV_BLOCK : first + (block + 1) * CONV_BLOCK] = result.astype(BF16)

        unroll = math.gcd(chunk // GROUP_SIZE, UNROLL)

        def some(step, carry):
            for i in range(unroll):
                one_group(step * unroll + i)
            return carry

        lax.fori_loop(0, chunk // GROUP_SIZE // unroll, some, 0)

    def turn_gate(p, j):
        first, size = starts[p], sizes[p]
        gate_t[:, :size] = gate_raw[first : first + size, at(j * chunk, chunk)].astype(F32).T

    def project(p):
        columns = slice(starts[p], starts[p] + sizes[p])

        def one(i, carry):
            owner = jnp.where(2 * z < ranges, last_range - i, i)
            start = at(owner * rows + core * half_rows, half_rows)
            total = jnp.dot(
                weights[0, start], mine[:, columns], preferred_element_type=F32
            ) + jnp.dot(weights[1, start], theirs[:, columns], preferred_element_type=F32)
            parts[p][at(owner * half_rows, half_rows)] = total.astype(BF16)

            @pl.when((z == 0) & (i == 0))
            def _():
                for m in range(2):
                    up_copy(p, owner, m).start()

            @pl.when((z == last_range) & (i == 0))
            def _():
                for m in range(2):
                    down_copy(p, owner, m, z - 1).start()

            return carry

        lax.fori_loop(0, ranges, one, 0)

    def send_halo(p, chunks):
        @pl.when(has_next & (core == homes[p]))
        def _():
            def one(i, carry):
                for side in range(2):
                    halo_copy(side, p, i).start()
                return carry

            lax.fori_loop(*chunks, one, 0)

    for p in range(passes):

        def conv_chunk(j, carry, p=p):
            @pl.when(j == 0)
            def _():
                pl.when(core == homes[p])(lambda: gate_local(p).wait())
                pl.when(core != homes[p])(lambda: gate_remote(p).wait_recv())
                if 0 < p < passes - 1:
                    send_gate(p + 1)

            turn_gate(p, j)
            if p == 0:
                pair_copy(j).wait_recv()

            @pl.when(has_previous)
            def _():
                halo_copy(0, p, j).wait_recv()

            if p == 0:
                pl.when((j > 0) & (j < CHUNKS - 1))(lambda: send_halo(1, (j - 1, j)))
                pl.when(j == CHUNKS - 1)(lambda: send_halo(1, (j - 1, j + 1)))
            elif p == 1:
                send_halo(p + 1, (j, j + 1))
            elif p < passes - 1:
                pl.when(j == CHUNKS - 1)(lambda: send_halo(p + 1, (0, CHUNKS)))
            if p > 0:
                forward_slot(p - 1, j)
            if p > 1:
                pl.when(j == 0)(lambda: finish(p - 2))
            convolve(p, j)
            gated_copy(p, j).start()
            return carry

        lax.fori_loop(0, CHUNKS, conv_chunk, 0)
        if p == 0:
            weight_local(0).wait()
            weight_local(1).wait()

        def gated_here(j, carry, p=p):
            gated_copy(p, j).wait_recv()
            return carry

        lax.fori_loop(0, CHUNKS, gated_here, 0)
        project(p)

    def last_slots(slot, carry):
        forward_slot(passes - 1, slot)
        pl.when(slot == CHUNKS // 2 - 1)(lambda: finish(passes - 2))
        return carry

    lax.fori_loop(0, CHUNKS, last_slots, 0)
    finish(passes - 1)

    for p in range(passes):
        pl.when(core == homes[p])(lambda: gate_remote(p).wait_send())

    def pairs_done(j, carry):
        pair_copy(j).wait_send()

        for p in range(passes):
            gated_copy(p, j).wait_send()

            @pl.when(has_next & (core == homes[p]))
            def _():
                for side in range(2):
                    halo_copy(side, p, j).wait_send()

        return carry

    lax.fori_loop(0, CHUNKS, pairs_done, 0)

    def sums_done(i, carry):
        owner, m = i // 2, i % 2
        for q in range(passes):

            @pl.when((owner > z) & ((z > 0) | (owner == 1)))
            def _():
                up_copy(q, owner, m).wait_send()

            @pl.when((owner < z) & ((z < last_range) | (owner == last_range - 1)))
            def _():
                down_copy(q, owner, m, z - 1).wait_send()

        return carry

    lax.fori_loop(0, 2 * ranges, sums_done, 0)
    for p in range(passes):
        for m in range(2):

            @pl.when(core == homes[p])
            def _():
                out_copy(p, m).wait()
                pair_out_copy(p, m, 1 - core).wait_recv()

            @pl.when(core != homes[p])
            def _():
                pair_out_copy(p, m, core).wait_send()


def solution(mesh):
    ranges = mesh.shape["tp"]
    chips = mesh.shape["seq"] // 2

    def body(gate_input, key_input, value_input, filter_taps, out_weight):
        tokens, width = gate_input.shape
        half = width // 2
        chunk = half // CHUNKS
        sizes = [2 * tokens * share // sum(SHARES) for share in SHARES]
        count = len(SHARES)
        length = filter_taps.shape[1]
        outputs = out_weight.shape[0]
        rows = outputs // ranges
        groups = half // GROUP_SIZE
        dma = pltpu.SemaphoreType.DMA
        return pl.pallas_call(
            functools.partial(kernel, ranges, chips),
            in_specs=[pl.BlockSpec(memory_space=pl.ANY)] * 5,
            out_specs=pl.BlockSpec(memory_space=pl.ANY),
            out_shape=jax.ShapeDtypeStruct((rows, tokens), BF16),
            scratch_shapes=[
                pltpu.VMEM((half, 4 * tokens), BF16),
                pltpu.VMEM((half, tokens), BF16),
                pltpu.VMEM((2 * tokens, half), BF16),
                pltpu.VMEM((half, 2 * tokens), BF16),
                pltpu.VMEM((half, 2 * tokens), BF16),
                pltpu.VMEM((2, outputs, half), BF16),
                pltpu.VMEM((groups, length), BF16),
                pltpu.VMEM((groups, length + LANES), F32),
                pltpu.VMEM((chunk, max(sizes)), F32),
                dma((2, 2, CHUNKS)),
                dma((4,)),
                dma((3, count)),
                dma((CHUNKS,)),
                dma((CHUNKS,)),
                dma((2, count, CHUNKS)),
                *[dma((count, CHUNKS))] * 3,
                *[dma((count, ranges, 2))] * 4,
                *[dma((count, 2))] * 3,
                *[pltpu.VMEM((outputs // 2, size), BF16) for size in sizes],
                *[pltpu.VMEM(((ranges + 1) * rows // 2, size), BF16) for size in sizes],
            ],
            compiler_params=pltpu.CompilerParams(
                collective_id=0, has_side_effects=True, vmem_limit_bytes=62 * 1024 * 1024
            ),
            cost_estimate=pl.CostEstimate(
                flops=2 * tokens * width * (length + outputs),
                bytes_accessed=2 * (3 * tokens * width + outputs * width + rows * tokens),
                transcendentals=0,
            ),
        )(gate_input, key_input, value_input, filter_taps, out_weight)

    return jax.shard_map(
        body,
        mesh=mesh,
        in_specs=(P("seq", "tp"), P("seq", "tp"), P("seq", "tp"), P("tp", None), P(None, "tp")),
        out_specs=P("tp", "seq"),
        check_vma=False,
    )
```

```python
import functools
import math

import jax
import jax.numpy as jnp
from jax import lax
from jax.experimental import pallas as pl
from jax.experimental.pallas import tpu as pltpu
from jax.sharding import PartitionSpec as P

GROUP_SIZE = 16
LANES = 128
BLOCK = 256
CONV_BLOCK = 128
CHUNKS = 4
UNROLL = 16
SHARES = (2, 3, 3, 4, 4)
MESH = pl.DeviceIdType.MESH
BF16 = jnp.bfloat16
F32 = jnp.float32


def at(start, size, multiple=None):
    return pl.ds(pl.multiple_of(start, multiple or size), size)


def kernel(
    ranges,
    chips,
    gate,
    key,
    value,
    taps,
    weight,
    out,
    signal,
    other,
    gate_raw,
    mine,
    theirs,
    weights,
    taps_raw,
    lines,
    gate_t,
    kv_sem,
    local_sem,
    gate_sem,
    pair_send,
    pair_recv,
    halo_send,
    halo_recv,
    gated_send,
    gated_recv,
    up_send,
    up_recv,
    down_send,
    down_recv,
    out_sem,
    pair_out_send,
    pair_out_recv,
    *sums,
):
    tokens, width = gate.shape
    half = width // 2
    passes = len(SHARES)
    parts, landeds = sums[:passes], sums[passes:]
    sizes = [2 * tokens * share // sum(SHARES) for share in SHARES]
    starts = [2 * tokens - sum(sizes[: p + 1]) for p in range(passes)]
    homes = [start // tokens for start in starts]
    chunk = half // CHUNKS
    length = taps.shape[1]
    groups = half // GROUP_SIZE
    rows = weight.shape[0] // ranges
    half_rows = rows // 2
    piece_rows = half_rows // 2
    place = lax.axis_index("seq")
    z = lax.axis_index("tp")
    chip = place // 2
    core = place % 2
    sibling = (chip * 2 + 1 - core, z)
    last_range = ranges - 1
    has_next = chip < chips - 1
    has_previous = chip > 0
    own_column = 2 * tokens + core * tokens

    def staged(which, side, j):
        return weights.at[which, at(j * tokens, tokens), side * chunk : (side + 1) * chunk]

    def load(which, side, j):
        column = (core if side == 0 else 1 - core) * half + j * chunk
        return pltpu.make_async_copy(
            (key, value)[which].at[:, at(column, chunk)],
            staged(which, side, j),
            kv_sem.at[which, side, j],
        )

    def gate_rows(p):
        return (
            slice(starts[p] % tokens, starts[p] % tokens + sizes[p]),
            slice(starts[p], starts[p] + sizes[p]),
        )

    def gate_local(p):
        here, there = gate_rows(p)
        return pltpu.make_async_copy(
            gate.at[here, at(core * half, half)], gate_raw.at[there], gate_sem.at[0, p]
        )

    def gate_remote(p):
        here, there = gate_rows(p)
        return pltpu.make_async_remote_copy(
            src_ref=gate.at[here, at((1 - core) * half, half)],
            dst_ref=gate_raw.at[there],
            send_sem=gate_sem.at[1, p],
            recv_sem=gate_sem.at[2, p],
            device_id=sibling,
            device_id_type=MESH,
        )

    def send_gate(p):
        @pl.when(core == homes[p])
        def _():
            gate_local(p).start()
            gate_remote(p).start()

    def taps_local():
        return pltpu.make_async_copy(
            taps.at[at(core * groups, groups)], taps_raw, local_sem.at[1]
        )

    def weight_local(side):
        column = (core if side == 0 else 1 - core) * half
        return pltpu.make_async_copy(
            weight.at[:, at(column, half)], weights.at[side], local_sem.at[2 + side]
        )

    def pair_copy(j):
        return pltpu.make_async_remote_copy(
            src_ref=other.at[at(j * chunk, chunk)],
            dst_ref=signal.at[at(j * chunk, chunk), at(own_column, tokens)],
            send_sem=pair_send.at[j],
            recv_sem=pair_recv.at[j],
            device_id=sibling,
            device_id_type=MESH,
        )

    def halo_copy(side, p, j):
        target = (chip + 1) * 2 + (core if side == 0 else 1 - core)
        start, size = starts[p], sizes[p]
        here = at(j * chunk, chunk)
        if side == 0:
            source = signal.at[here, 2 * tokens + start : 2 * tokens + start + size]
        else:
            source = other.at[here, start % tokens : start % tokens + size]
        return pltpu.make_async_remote_copy(
            src_ref=source,
            dst_ref=signal.at[here, start : start + size],
            send_sem=halo_send.at[side, p, j],
            recv_sem=halo_recv.at[p, j],
            device_id=(target, z),
            device_id_type=MESH,
        )

    def gated_copy(p, j):
        here = (at(j * chunk, chunk), slice(starts[p], starts[p] + sizes[p]))
        return pltpu.make_async_remote_copy(
            src_ref=mine.at[here],
            dst_ref=theirs.at[here],
            send_sem=gated_send.at[p, j],
            recv_sem=gated_recv.at[p, j],
            device_id=sibling,
            device_id_type=MESH,
        )

    def spot(owner, m):
        return at(owner * half_rows + m * piece_rows, piece_rows)

    def part_at(p, owner, m):
        return parts[p].at[spot(owner, m)]

    def up_copy(q, owner, m):
        return pltpu.make_async_remote_copy(
            src_ref=part_at(q, owner, m),
            dst_ref=landeds[q].at[spot(owner, m)],
            send_sem=up_send.at[q, owner, m],
            recv_sem=up_recv.at[q, owner, m],
            device_id=(place, z + 1),
            device_id_type=MESH,
        )

    def down_slot(owner, receiver):
        return jnp.where(owner == receiver, ranges, owner)

    def down_copy(q, owner, m, receiver):
        return pltpu.make_async_remote_copy(
            src_ref=part_at(q, owner, m),
            dst_ref=landeds[q].at[spot(down_slot(owner, receiver), m)],
            send_sem=down_send.at[q, owner, m],
            recv_sem=down_recv.at[q, owner, m],
            device_id=(place, z - 1),
            device_id_type=MESH,
        )

    def out_at(p, writer, m):
        column = starts[p] % tokens
        return out.at[
            at(writer * half_rows + m * piece_rows, piece_rows), column : column + sizes[p]
        ]

    def out_copy(p, m):
        return pltpu.make_async_copy(part_at(p, z, m), out_at(p, core, m), out_sem.at[p, m])

    def pair_out_copy(p, m, writer):
        return pltpu.make_async_remote_copy(
            src_ref=part_at(p, z, m),
            dst_ref=out_at(p, writer, m),
            send_sem=pair_out_send.at[p, m],
            recv_sem=pair_out_recv.at[p, m],
            device_id=sibling,
            device_id_type=MESH,
        )

    def arrived(q, slot, m):
        return landeds[q][spot(slot, m)].astype(F32)

    def mine_of(q, owner, m):
        return parts[q][spot(owner, m)].astype(F32)

    def put(q, owner, m, total):
        parts[q][spot(owner, m)] = total.astype(BF16)

    def add(q, owner, m):
        put(q, owner, m, mine_of(q, owner, m) + arrived(q, owner, m))

    def forward(q, step):
        upper_item = jnp.maximum(step - 2 * z, 0)
        upper = last_range - upper_item // 2
        lower_item = jnp.maximum(step - 2 * (last_range - z), 0)
        lower = lower_item // 2

        @pl.when((step >= 2 * z) & (upper > z))
        def _():
            m = upper_item % 2

            @pl.when(z == 0)
            def _():
                up_copy(q, upper + 1, m).wait_send()

            @pl.when(z > 0)
            def _():
                up_copy(q, upper, m).wait_recv()
                add(q, upper, m)

            up_copy(q, upper, m).start()

        @pl.when((step >= 2 * (last_range - z)) & (lower < z))
        def _():
            m = lower_item % 2

            @pl.when(z == last_range)
            def _():
                down_copy(q, lower - 1, m, z - 1).wait_send()

            @pl.when(z < last_range)
            def _():
                down_copy(q, lower, m, z).wait_recv()
                add(q, lower, m)

            down_copy(q, lower, m, z - 1).start()

    items = 2 * (ranges - 2)

    def forward_slot(q, slot):
        def one(i, carry):
            forward(q, i + 2)
            return carry

        lax.fori_loop(slot * items // CHUNKS, (slot + 1) * items // CHUNKS, one, 0)

    def finish(q):
        def one(m, carry):
            @pl.when(z > 0)
            def _():
                up_copy(q, z, m).wait_recv()

            @pl.when(z < last_range)
            def _():
                down_copy(q, z, m, z).wait_recv()

            @pl.when(z == 0)
            def _():
                put(q, z, m, mine_of(q, z, m) + arrived(q, ranges, m))

            @pl.when((z > 0) & (z < last_range))
            def _():
                put(q, z, m, mine_of(q, z, m) + arrived(q, z, m) + arrived(q, ranges, m))

            @pl.when(z == last_range)
            def _():
                put(q, z, m, mine_of(q, z, m) + arrived(q, z, m))

            pl.when(core == homes[q])(lambda: out_copy(q, m).start())
            pl.when(core != homes[q])(lambda: pair_out_copy(q, m, core).start())
            return carry

        lax.fori_loop(0, 2, one, 0)

    barrier = pltpu.get_barrier_semaphore()

    def greet(device):
        pl.semaphore_signal(barrier, inc=1, device_id=device, device_id_type=MESH)

    for j in range(CHUNKS):
        for side in range(2):
            load(0, side, j).start()
            load(1, side, j).start()
    taps_local().start()
    greet(sibling)

    @pl.when(has_previous)
    def _():
        greet((place - 2, z))
        greet((chip * 2 - 1 - core, z))

    @pl.when(has_next)
    def _():
        greet((place + 2, z))
        greet((chip * 2 + 3 - core, z))

    @pl.when(z > 0)
    def _():
        greet((place, z - 1))

    @pl.when(z < last_range)
    def _():
        greet((place, z + 1))

    one = lambda flag: jnp.where(flag, 1, 0)
    peers = 1 + 2 * one(has_previous) + 2 * one(has_next) + one(z > 0) + one(z < last_range)
    pl.semaphore_wait(barrier, peers)

    def product_chunk(j, carry):
        for side in range(2):
            load(0, side, j).wait()
            load(1, side, j).wait()
            for block in range(tokens // BLOCK):
                span = slice(block * BLOCK, (block + 1) * BLOCK)
                here = at(j * tokens + block * BLOCK, BLOCK)
                column = slice(side * chunk, (side + 1) * chunk)
                product = weights[0, here, column].astype(F32) * weights[1, here, column].astype(F32)
                turned = product.T.astype(BF16)
                if side == 0:
                    signal[at(j * chunk, chunk), at(own_column + block * BLOCK, BLOCK)] = turned
                else:
                    other[at(j * chunk, chunk), span] = turned

            if side == 1:
                pair_copy(j).start()

            @pl.when(has_next & (core == 1))
            def _():
                halo_copy(side, 0, j).start()

        return carry

    send_gate(0)
    lax.fori_loop(0, CHUNKS, product_chunk, 0)
    send_gate(1)
    weight_local(0).start()
    weight_local(1).start()
    taps_local().wait()
    lines[:, :length] = taps_raw[...].astype(F32)
    lines[:, length:] = jnp.zeros((groups, LANES), F32)

    @pl.when(jnp.logical_not(has_previous))
    def _():
        signal[:, : 2 * tokens] = jnp.zeros((half, 2 * tokens), BF16)

    per_block = CONV_BLOCK // LANES
    lag_tiles = length // LANES
    lag_blocks = lag_tiles + per_block

    def convolve(p, j):
        first = starts[p]
        blocks = sizes[p] // CONV_BLOCK
        window = 2 * tokens + first - length
        empty = jnp.zeros((LANES, LANES), BF16)

        def one_group(local):
            group = j * (chunk // GROUP_SIZE) + local
            here = at(group * GROUP_SIZE, GROUP_SIZE)
            left = jnp.concatenate(
                [
                    jnp.concatenate(
                        [
                            signal[
                                here,
                                window + block * CONV_BLOCK + lag * LANES : window
                                + block * CONV_BLOCK
                                + (lag + 1) * LANES,
                            ]
                            for block in range(blocks)
                        ],
                        axis=0,
                    )
                    for lag in range(lag_blocks)
                ],
                axis=1,
            )
            line = lines[pl.ds(group, 1), :]
            spread = jnp.broadcast_to(line, (LANES, line.shape[1]))
            band = pltpu.roll(spread, 0, 1, stride=1, stride_axis=0).astype(BF16)

            def tile(index):
                if index < 0 or index > lag_tiles:
                    return empty
                return band[:, index * LANES : (index + 1) * LANES]

            matrix = jnp.concatenate(
                [
                    jnp.concatenate(
                        [tile(lag_tiles + across - lag) for across in range(per_block)], axis=1
                    )
                    for lag in range(lag_blocks)
                ],
                axis=0,
            )
            conv = jnp.dot(left, matrix, preferred_element_type=F32)
            local_rows = at(local * GROUP_SIZE, GROUP_SIZE)
            for block in range(blocks):
                columns = slice(block * CONV_BLOCK, (block + 1) * CONV_BLOCK)
                result = gate_t[local_rows, columns] * conv[
                    block * GROUP_SIZE : (block + 1) * GROUP_SIZE
                ]
                mine[here, first + block * CONV_BLOCK : first + (block + 1) * CONV_BLOCK] = result.astype(BF16)

        unroll = math.gcd(chunk // GROUP_SIZE, UNROLL)

        def some(step, carry):
            for i in range(unroll):
                one_group(step * unroll + i)
            return carry

        lax.fori_loop(0, chunk // GROUP_SIZE // unroll, some, 0)

    def turn_gate(p, j):
        first, size = starts[p], sizes[p]
        gate_t[:, :size] = gate_raw[first : first + size, at(j * chunk, chunk)].astype(F32).T

    def project(p):
        columns = slice(starts[p], starts[p] + sizes[p])

        def one(i, carry):
            owner = jnp.where(2 * z < ranges, last_range - i, i)
            start = at(owner * rows + core * half_rows, half_rows)
            total = jnp.dot(
                weights[0, start], mine[:, columns], preferred_element_type=F32
            ) + jnp.dot(weights[1, start], theirs[:, columns], preferred_element_type=F32)
            parts[p][at(owner * half_rows, half_rows)] = total.astype(BF16)

            @pl.when((z == 0) & (i == 0))
            def _():
                for m in range(2):
                    up_copy(p, owner, m).start()

            @pl.when((z == last_range) & (i == 0))
            def _():
                for m in range(2):
                    down_copy(p, owner, m, z - 1).start()

            return carry

        lax.fori_loop(0, ranges, one, 0)

    def send_halo(p, chunks):
        @pl.when(has_next & (core == homes[p]))
        def _():
            def one(i, carry):
                for side in range(2):
                    halo_copy(side, p, i).start()
                return carry

            lax.fori_loop(*chunks, one, 0)

    for p in range(passes):

        def conv_chunk(j, carry, p=p):
            @pl.when(j == 0)
            def _():
                pl.when(core == homes[p])(lambda: gate_local(p).wait())
                pl.when(core != homes[p])(lambda: gate_remote(p).wait_recv())
                if 0 < p < passes - 1:
                    send_gate(p + 1)

            turn_gate(p, j)
            if p == 0:
                pair_copy(j).wait_recv()

            @pl.when(has_previous)
            def _():
                halo_copy(0, p, j).wait_recv()

            if p == 0:
                pl.when((j > 0) & (j < CHUNKS - 1))(lambda: send_halo(1, (j - 1, j)))
                pl.when(j == CHUNKS - 1)(lambda: send_halo(1, (j - 1, j + 1)))
            elif p == 1:
                send_halo(p + 1, (j, j + 1))
            elif p < passes - 1:
                pl.when(j == CHUNKS - 1)(lambda: send_halo(p + 1, (0, CHUNKS)))
            if p > 0:
                forward_slot(p - 1, j)
            if p > 1:
                pl.when(j == CHUNKS - 1)(lambda: finish(p - 2))
            convolve(p, j)
            gated_copy(p, j).start()
            return carry

        lax.fori_loop(0, CHUNKS, conv_chunk, 0)
        if p == 0:
            weight_local(0).wait()
            weight_local(1).wait()

        def gated_here(j, carry, p=p):
            gated_copy(p, j).wait_recv()
            return carry

        lax.fori_loop(0, CHUNKS, gated_here, 0)
        project(p)

    def last_slots(slot, carry):
        forward_slot(passes - 1, slot)
        pl.when(slot == CHUNKS // 2 - 1)(lambda: finish(passes - 2))
        return carry

    lax.fori_loop(0, CHUNKS, last_slots, 0)
    finish(passes - 1)

    for p in range(passes):
        pl.when(core == homes[p])(lambda: gate_remote(p).wait_send())

    def pairs_done(j, carry):
        pair_copy(j).wait_send()

        for p in range(passes):
            gated_copy(p, j).wait_send()

            @pl.when(has_next & (core == homes[p]))
            def _():
                for side in range(2):
                    halo_copy(side, p, j).wait_send()

        return carry

    lax.fori_loop(0, CHUNKS, pairs_done, 0)

    def sums_done(i, carry):
        owner, m = i // 2, i % 2
        for q in range(passes):

            @pl.when((owner > z) & ((z > 0) | (owner == 1)))
            def _():
                up_copy(q, owner, m).wait_send()

            @pl.when((owner < z) & ((z < last_range) | (owner == last_range - 1)))
            def _():
                down_copy(q, owner, m, z - 1).wait_send()

        return carry

    lax.fori_loop(0, 2 * ranges, sums_done, 0)
    for p in range(passes):
        for m in range(2):

            @pl.when(core == homes[p])
            def _():
                out_copy(p, m).wait()
                pair_out_copy(p, m, 1 - core).wait_recv()

            @pl.when(core != homes[p])
            def _():
                pair_out_copy(p, m, core).wait_send()


def solution(mesh):
    ranges = mesh.shape["tp"]
    chips = mesh.shape["seq"] // 2

    def body(gate_input, key_input, value_input, filter_taps, out_weight):
        tokens, width = gate_input.shape
        half = width // 2
        chunk = half // CHUNKS
        sizes = [2 * tokens * share // sum(SHARES) for share in SHARES]
        count = len(SHARES)
        length = filter_taps.shape[1]
        outputs = out_weight.shape[0]
        rows = outputs // ranges
        groups = half // GROUP_SIZE
        dma = pltpu.SemaphoreType.DMA
        return pl.pallas_call(
            functools.partial(kernel, ranges, chips),
            in_specs=[pl.BlockSpec(memory_space=pl.ANY)] * 5,
            out_specs=pl.BlockSpec(memory_space=pl.ANY),
            out_shape=jax.ShapeDtypeStruct((rows, tokens), BF16),
            scratch_shapes=[
                pltpu.VMEM((half, 4 * tokens), BF16),
                pltpu.VMEM((half, tokens), BF16),
                pltpu.VMEM((2 * tokens, half), BF16),
                pltpu.VMEM((half, 2 * tokens), BF16),
                pltpu.VMEM((half, 2 * tokens), BF16),
                pltpu.VMEM((2, outputs, half), BF16),
                pltpu.VMEM((groups, length), BF16),
                pltpu.VMEM((groups, length + LANES), F32),
                pltpu.VMEM((chunk, max(sizes)), F32),
                dma((2, 2, CHUNKS)),
                dma((4,)),
                dma((3, count)),
                dma((CHUNKS,)),
                dma((CHUNKS,)),
                dma((2, count, CHUNKS)),
                *[dma((count, CHUNKS))] * 3,
                *[dma((count, ranges, 2))] * 4,
                *[dma((count, 2))] * 3,
                *[pltpu.VMEM((outputs // 2, size), BF16) for size in sizes],
                *[pltpu.VMEM(((ranges + 1) * rows // 2, size), BF16) for size in sizes],
            ],
            compiler_params=pltpu.CompilerParams(
                collective_id=0, has_side_effects=True, vmem_limit_bytes=62 * 1024 * 1024
            ),
            cost_estimate=pl.CostEstimate(
                flops=2 * tokens * width * (length + outputs),
                bytes_accessed=2 * (3 * tokens * width + outputs * width + rows * tokens),
                transcendentals=0,
            ),
        )(gate_input, key_input, value_input, filter_taps, out_weight)

    return jax.shard_map(
        body,
        mesh=mesh,
        in_specs=(P("seq", "tp"), P("seq", "tp"), P("seq", "tp"), P("tp", None), P(None, "tp")),
        out_specs=P("tp", "seq"),
        check_vma=False,
    )
```
